256 devices in a mesh: silo: 32 (over z, y_lo, core), shard: 8 (over x, y_hi).
Axes of the slice: x: 4, y: 4 (y_hi: 2, y_lo: 2; y = y_hi * 2 + y_lo), z: 8, core: 2. Of those that a mesh axis runs over, the one named last changes fastest.
Arguments:
- activ: bfloat16 [262144, 1280], P(('silo', 'shard')), may hold values from -6 to 6
- cotangent: bfloat16 [262144, 640], P(('silo', 'shard')), may hold values from -6 to 6
- error_memory: float32 [32, 8, 3200, 256], P('silo', 'shard'), may hold values from -5 to 5
- params: float32 [32, 640, 1280], P('silo', 'shard'), may hold values from -6 to 6
- estimate: float32 [32, 640, 1280], P('silo', 'shard'), may hold values from -6 to 6
- mixed: float32 [32, 640, 1280], P('silo', 'shard'), may hold values from -6 to 6
- kept_blocks: int32 [32, 8, 8, 64], P('silo'), may hold values from 0 to 399, as said below
- kept_counts: int32 [32, 8, 8], P('silo'), may hold values from 1 to 64, as said below
- gossip_blocks: int32 [32, 8, 128], P(None, 'shard'), may hold values from 0 to 399, as said below
- gossip_counts: int32 [32, 8], P(None, 'shard'), may hold values from 1 to 128, as said below
Outputs:
- params_out: float32 [32, 640, 1280], P('silo', 'shard')
- estimate_out: float32 [32, 640, 1280], P('silo', 'shard')
- mixed_out: float32 [32, 640, 1280], P('silo', 'shard')
- error_out: float32 [32, 8, 3200, 256], P('silo', 'shard')
The draws below stay inside these ranges and needn't reach their ends.
Inputs may be any that keep to these rules, and one draw needn't show every extreme that they name: `kept_blocks`: for each silo, sender and owner the 64 entries are distinct. In every silo some owner has kept_counts equal to 64 from every sender. `kept_counts`: in every silo one owner receives 64 from every device of the silo. `gossip_blocks`: for each silo and owner the 128 entries are distinct. `gossip_counts`: for every owner some silo gossips 128 blocks.
All inputs are finite; a program needn't handle non-finite values.
Results may differ from the reference program's by a relative error of at most 0.0003.
Values sent between devices are 32-bit elements; how exact they have to be, the bound alone decides.
A program may use at most 64 MiB of HBM per device.

```python
import jax
import jax.numpy as jnp
from jax import lax

C_IN = 1280
C_OUT = 640
BLK = 256
TOK_DEV = 1024
CAP = 64
GK = 128
SILOS = 32
SHARDS = 8
NB = 3200
BLK_OWN = 400
ROWS = 262144


def distinct_lists(key, groups, length):
    keys = jax.random.split(key, groups)
    rows = jax.vmap(lambda one_key: jax.random.permutation(one_key, BLK_OWN)[:length])(keys)
    return rows.astype(jnp.int32)


def draw_kept_blocks(key, part):
    rows = distinct_lists(jax.random.fold_in(key, 11), SILOS * SHARDS * SHARDS, CAP)
    return rows.reshape(SILOS, SHARDS, SHARDS, CAP)


def draw_kept_counts(key, part):
    key_heat, key_base, key_full = jax.random.split(jax.random.fold_in(key, 23), 3)
    heat = jax.random.randint(key_heat, (SILOS, 1, SHARDS), 1, 5)
    base = jax.random.randint(key_base, (SILOS, SHARDS, SHARDS), 0, CAP)
    counts = jnp.clip(base * heat // 2 + 1, 1, CAP)
    hottest = jax.random.randint(key_full, (SILOS,), 0, SHARDS)
    full_owner = jnp.arange(SHARDS)[None, None, :] == hottest[:, None, None]
    return jnp.where(full_owner, CAP, counts).astype(jnp.int32)


def draw_gossip_blocks(key, part):
    rows = distinct_lists(jax.random.fold_in(key, 37), SILOS * SHARDS, GK)
    return rows.reshape(SILOS, SHARDS, GK)


def draw_gossip_counts(key, part):
    key_base, key_full = jax.random.split(jax.random.fold_in(key, 41), 2)
    counts = jax.random.randint(key_base, (SILOS, SHARDS), 1, GK + 1)
    fullest = jax.random.randint(key_full, (SHARDS,), 0, SILOS)
    full_silo = jnp.arange(SILOS)[:, None] == fullest[None, :]
    return jnp.where(full_silo, GK, counts).astype(jnp.int32)


def levels(own_key, dims, cuts, low, largest):
    level = 1.0
    for position, shards_of in cuts:
        draws = jax.random.uniform(jax.random.fold_in(jax.random.fold_in(own_key, 6), position), (shards_of,), jnp.float32, low / len(cuts), largest / len(cuts))
        level = level * jnp.repeat(jnp.exp(draws), dims[position] // shards_of).reshape((-1,) + (1,) * (len(dims) - 1 - position))
    return level


def scatter_about(key, extent, scale, reach, shards=(), held_as=jnp.bfloat16):
    loudness = levels(key, extent, shards, -0.22, 0.18) if shards else 1.0
    values = jax.random.normal(key, extent, jnp.float32) * scale * loudness
    return jnp.minimum(jnp.maximum(values, -reach), reach).astype(held_as)


def setup_inputs(seed: int = 0) -> dict:
    splits = jax.random.split(jax.random.key(seed), 11)
    activ = scatter_about(splits[0], (ROWS, C_IN), 1.0, 6.0, ((0, 256),))
    cotangent = scatter_about(splits[1], (ROWS, C_OUT), 1.0, 6.0, ((0, 256),))
    error_memory = scatter_about(splits[2], (SILOS, SHARDS, NB, BLK), 0.7, 5.0, ((0, 32), (1, 8)), jnp.float32)
    params = scatter_about(splits[3], (SILOS, C_OUT, C_IN), 1.0, 6.0, ((0, 32), (1, 8)), jnp.float32)
    estimate = scatter_about(splits[4], (SILOS, C_OUT, C_IN), 1.0, 6.0, ((0, 32), (1, 8)), jnp.float32)
    mixed = scatter_about(splits[5], (SILOS, C_OUT, C_IN), 1.0, 6.0, ((0, 32), (1, 8)), jnp.float32)
    kept_blocks = draw_kept_blocks(jax.random.fold_in(splits[10], 71), 0)
    kept_counts = draw_kept_counts(jax.random.fold_in(splits[10], 71), 0)
    gossip_blocks = draw_gossip_blocks(jax.random.fold_in(splits[10], 71), 0)
    gossip_counts = draw_gossip_counts(jax.random.fold_in(splits[10], 71), 0)
    return {"activ": activ, "cotangent": cotangent, "error_memory": error_memory, "params": params, "estimate": estimate, "mixed": mixed, "kept_blocks": kept_blocks, "kept_counts": kept_counts, "gossip_blocks": gossip_blocks, "gossip_counts": gossip_counts}


LEARN_RATE = 0.25
CONSENSUS = 0.5
MIX_WEIGHT = 1.0 / 3.0


def reference(activ, cotangent, error_memory, params, estimate, mixed, kept_blocks, kept_counts, gossip_blocks, gossip_counts):
    scale_in = C_IN ** -0.5
    acts = activ.reshape(SILOS, SHARDS, TOK_DEV, C_IN)
    cots = cotangent.reshape(SILOS, SHARDS, TOK_DEV, C_OUT)
    offsets = (jnp.arange(SHARDS, dtype=jnp.int32) * BLK_OWN)[:, None]
    slot_ids = jnp.arange(CAP, dtype=jnp.int32)[None, :]
    gossip_slot_ids = jnp.arange(GK, dtype=jnp.int32)[None, :]

    def one_device(inputs):
        act_rows, cot_rows, memory, my_lists, my_counts = inputs
        grad_local = jnp.dot(cot_rows.T, act_rows, preferred_element_type=jnp.float32) * scale_in
        pending = memory + grad_local.reshape(NB, BLK)
        global_ids = (my_lists + offsets).reshape(-1)
        filled = (slot_ids < my_counts[:, None]).astype(jnp.int32).reshape(-1)
        chosen = jnp.zeros((NB,), jnp.int32).at[global_ids].max(filled)
        keep_mask = chosen[:, None] > 0
        return jnp.where(keep_mask, jnp.float32(0.0), pending), jnp.where(keep_mask, pending, jnp.float32(0.0))

    def one_silo(inputs):
        act_silo, cot_silo, memory_silo, lists_silo, counts_silo, weights_silo, estimate_silo, gossip_silo, gcounts_silo = inputs
        error_part, kept_terms = lax.map(one_device, (act_silo, cot_silo, memory_silo, lists_silo, counts_silo))
        summed = jnp.sum(kept_terms, axis=0)
        half_step = weights_silo.reshape(NB, BLK) - LEARN_RATE * summed
        drift = half_step - estimate_silo.reshape(NB, BLK)
        gossip_ids = (gossip_silo + offsets).reshape(-1)
        gossip_filled = (gossip_slot_ids < gcounts_silo[:, None]).astype(jnp.int32).reshape(-1)
        gossip_chosen = jnp.zeros((NB,), jnp.int32).at[gossip_ids].max(gossip_filled)
        delta = jnp.where(gossip_chosen[:, None] > 0, drift, jnp.float32(0.0))
        return error_part, half_step, delta

    error_out, half_step, delta = lax.map(one_silo, (acts, cots, error_memory, kept_blocks, kept_counts, params, estimate, gossip_blocks, gossip_counts))
    estimate_out = estimate + delta.reshape(estimate.shape)
    spread = delta + jnp.roll(delta, 1, axis=0) + jnp.roll(delta, -1, axis=0)
    mixed_out = mixed + MIX_WEIGHT * spread.reshape(mixed.shape)
    params_out = half_step.reshape(params.shape) + CONSENSUS * (mixed_out - estimate_out)
    return params_out, estimate_out, mixed_out, error_out
```

```python
import functools

import jax
import jax.numpy as jnp
from jax import lax
from jax.experimental import pallas as pl
from jax.experimental.pallas import tpu as pltpu
from jax.sharding import PartitionSpec as P

LEARN_RATE = 0.25
CONSENSUS = 0.5
MIX_WEIGHT = 1.0 / 3.0
MESH = pl.DeviceIdType.MESH
LANES = 128


def split_pair(value):
    high = value.astype(jnp.bfloat16)
    low = (value - high.astype(jnp.float32)).astype(jnp.bfloat16)
    return high, low


def remote(src, dst, send, recv, target):
    return pltpu.make_async_remote_copy(
        src_ref=src, dst_ref=dst, send_sem=send, recv_sem=recv,
        device_id=target, device_id_type=MESH,
    )


def kernel(
    dims,
    activ_h, cot_h, mem_h, params_h, est_h, mixed_h, kept_h, kcnt_h, gos_h, gcnt_h,
    params_o, est_o, mixed_o, error_o,
    act_v, cot_v, cot_t, pend, slots, arrived, pieces, onehot, mask_own, gos_take, gos_put,
    drift_p, gos_send, gos_recv, gos_p, par_v, est_v, mix_v, kept_v, gos_v,
    kept_s, kcnt_s, gcnt_s,
    load_sem, send_sem, recv_sem, gsend_sem, grecv_sem,
):
    silos, shards, own, cap, gk, tiles, block = dims
    rows = own // tiles
    halves = block // LANES
    total_rows = rows * shards
    silo = lax.axis_index("silo")
    shard = lax.axis_index("shard")
    upper = lax.rem(silo + 1, silos)
    lower = lax.rem(silo + silos - 1, silos)
    scale = float(act_v.shape[1]) ** -0.5

    loads = []

    def load(src, dst):
        copy = pltpu.make_async_copy(src, dst, load_sem.at[len(loads)])
        copy.start()
        loads.append(copy)
        return copy

    load_cot = load(cot_h, cot_v)
    load_act = [
        load(activ_h.at[:, pl.ds(c * block, block)], act_v.at[:, pl.ds(c * block, block)])
        for c in range(tiles)
    ]
    load_mem = [load(mem_h.at[:, pl.ds(h * LANES, LANES)], pend.at[h]) for h in range(halves)]
    load_kept_s = load(kept_h.at[shard], kept_s)
    load_rest = [
        load(kept_h, kept_v),
        load(kcnt_h, kcnt_s),
        load(gos_h, gos_v),
        load(gcnt_h, gcnt_s),
        load(params_h, par_v),
        load(est_h, est_v),
        load(mixed_h, mix_v),
    ]

    barrier = pltpu.get_barrier_semaphore()
    for step in range(1, shards):
        pl.semaphore_signal(
            barrier, inc=1, device_id=(silo, lax.rem(shard + step, shards)), device_id_type=MESH
        )
    for other in (lower, upper):
        pl.semaphore_signal(barrier, inc=1, device_id=(other, shard), device_id_type=MESH)

    load_cot.wait()
    cot_t[...] = cot_v[...].T
    for copy in load_mem:
        copy.wait()
    for c in range(tiles):
        load_act[c].wait()
        grad = (
            jnp.dot(
                cot_t[...], act_v[:, pl.ds(c * block, block)], preferred_element_type=jnp.float32
            )
            * scale
        )
        for h in range(halves):
            view = pl.ds(c, total_rows, stride=tiles)
            pend[h, view, :] = pend[h, view, :] + grad[:, h * LANES : (h + 1) * LANES]

    load_kept_s.wait()
    pl.semaphore_wait(barrier, shards + 1)

    def gather(owner):
        def take(k, carry):
            row = owner * own + kept_s[owner, k]
            for h in range(halves):
                slots[owner, h, pl.ds(k, 1), :] = pend[h, pl.ds(row, 1), :]
            return carry

        lax.fori_loop(0, cap, take, 0, unroll=8)

    sends = []
    for step in list(range(1, shards)) + [0]:
        owner = lax.rem(shard + step, shards)
        gather(owner)
        if step:
            copy = remote(
                slots.at[owner], arrived.at[shard], send_sem.at[step], recv_sem.at[step],
                (silo, owner),
            )
            copy.start()
            sends.append(copy)
        else:
            arrived[shard] = slots[shard]

    for copy in load_rest:
        copy.wait()

    lane_cap = lax.broadcasted_iota(jnp.int32, (1, cap), 1)
    lane_gk = lax.broadcasted_iota(jnp.int32, (1, gk), 1)

    order = lax.broadcasted_iota(jnp.int32, (own, 1), 0)
    block_of = lax.rem(order, rows) * tiles + lax.div(order, rows)
    for pair in range(shards // 2):
        ids = []
        for source in (2 * pair, 2 * pair + 1):
            filled = lane_cap < kcnt_s[source, shard]
            ids.append(jnp.where(filled, kept_v[source, pl.ds(shard, 1), :], -1))
        ids = jnp.concatenate(ids, axis=1)
        onehot[:, pl.ds(pair * 2 * cap, 2 * cap)] = jnp.where(block_of == ids, 1.0, 0.0).astype(
            jnp.bfloat16
        )

    def gossip_hot(which):
        ids = jnp.where(lane_gk < gcnt_s[0, which], gos_v[which], -1)
        return jnp.where(block_of == ids, 1.0, 0.0)

    mine = gossip_hot(silo)
    ones = jnp.ones((gk, LANES), jnp.bfloat16)
    mask_own[...] = jnp.dot(mine.astype(jnp.bfloat16), ones, preferred_element_type=jnp.float32)
    gos_take[...] = mine.T.astype(jnp.bfloat16)
    gos_put[:, pl.ds(0, gk)] = gossip_hot(lower).astype(jnp.bfloat16)
    gos_put[:, pl.ds(gk, gk)] = gossip_hot(upper).astype(jnp.bfloat16)

    ones_cap = jnp.ones((cap, LANES), jnp.bfloat16)
    place = lax.broadcasted_iota(jnp.int32, (own, 1), 0)

    def clear(owner, carry):
        ids = jnp.where(
            lane_cap < kcnt_s[shard, owner], kept_v[shard, pl.ds(owner, 1), :], -1
        )
        hit = jnp.where(place == ids, 1.0, 0.0).astype(jnp.bfloat16)
        kept = jnp.dot(hit, ones_cap, preferred_element_type=jnp.float32)
        base = pl.multiple_of(owner * own, 8)
        for h in range(halves):
            error_o[pl.ds(base, own), pl.ds(h * LANES, LANES)] = jnp.where(
                kept > 0.0, 0.0, pend[h, pl.ds(base, own), :]
            )
        return carry

    lax.fori_loop(0, shards, clear, 0)

    for copy in sends:
        copy.wait()

    slot_rows = shards * cap
    for h in range(halves):
        high, low = split_pair(arrived[:, h].reshape(slot_rows, LANES))
        pieces[:, pl.ds(h * LANES, LANES)] = high
        pieces[:, pl.ds(block + h * LANES, LANES)] = low
    for c in range(tiles):
        part = pl.ds(c * rows, rows)
        cols = pl.ds(c * block, block)
        added = jnp.dot(onehot[part, :], pieces[...], preferred_element_type=jnp.float32)
        half = par_v[:, cols] - LEARN_RATE * (added[:, :block] + added[:, block:])
        drift = half - est_v[:, cols]
        high, low = split_pair(drift)
        drift_p[part, pl.ds(0, block)] = high
        drift_p[part, pl.ds(block, block)] = low
        mask = mask_own[part, :] > 0.0
        delta = jnp.where(jnp.concatenate([mask] * halves, axis=1), drift, 0.0)
        estimate = est_v[:, cols] + delta
        est_o[:, cols] = estimate
        mix_v[:, cols] = mix_v[:, cols] + MIX_WEIGHT * delta
        par_v[:, cols] = half - CONSENSUS * estimate

    taken = jnp.dot(gos_take[...], drift_p[...], preferred_element_type=jnp.float32)
    gos_send[...] = taken[:, :block] + taken[:, block:]
    goes = [
        remote(gos_send, gos_recv.at[0], gsend_sem.at[0], grecv_sem.at[0], (upper, shard)),
        remote(gos_send, gos_recv.at[1], gsend_sem.at[1], grecv_sem.at[1], (lower, shard)),
    ]
    for copy in goes:
        copy.start()
    for copy in goes:
        copy.wait()
    high, low = split_pair(gos_recv[...].reshape(2 * gk, block))
    gos_p[:, pl.ds(0, block)] = high
    gos_p[:, pl.ds(block, block)] = low
    for c in range(tiles):
        cols = pl.ds(c * block, block)
        near = jnp.dot(
            gos_put[pl.ds(c * rows, rows), :], gos_p[...], preferred_element_type=jnp.float32
        )
        mixed = mix_v[:, cols] + MIX_WEIGHT * (near[:, :block] + near[:, block:])
        mixed_o[:, cols] = mixed
        params_o[:, cols] = par_v[:, cols] + CONSENSUS * mixed


def body(
    activ, cotangent, error_memory, params, estimate, mixed,
    kept_blocks, kept_counts, gossip_blocks, gossip_counts,
):
    silos, shards = lax.axis_size("silo"), lax.axis_size("shard")
    tokens, width_in = activ.shape
    width_out = cotangent.shape[1]
    nblocks, block = error_memory.shape[2:]
    own = nblocks // shards
    cap, gk = kept_blocks.shape[3], gossip_blocks.shape[2]
    tiles = width_in // block
    halves = block // LANES
    rows = own // tiles
    f32, bf16, i32 = jnp.float32, jnp.bfloat16, jnp.int32
    dims = (silos, shards, own, cap, gk, tiles, block)
    operands = (
        activ, cotangent, error_memory[0, 0], params[0], estimate[0], mixed[0],
        kept_blocks[0], kept_counts[0], gossip_blocks, gossip_counts.reshape(1, silos),
    )
    operands = tuple(pltpu.with_memory_space_constraint(x, pltpu.HBM) for x in operands)
    vmem = pltpu.VMEM
    outs = pl.pallas_call(
        functools.partial(kernel, dims),
        out_shape=(
            vmem((rows, width_in), f32),
            vmem((rows, width_in), f32),
            vmem((rows, width_in), f32),
            vmem((nblocks, block), f32),
        ),
        in_specs=[pl.BlockSpec(memory_space=pltpu.HBM)] * len(operands),
        out_specs=tuple([pl.BlockSpec(memory_space=pltpu.VMEM)] * 4),
        scratch_shapes=[
            vmem((tokens, width_in), bf16),
            vmem((tokens, width_out), bf16),
            vmem((width_out, tokens), bf16),
            vmem((halves, nblocks, LANES), f32),
            vmem((shards, halves, cap, LANES), f32),
            vmem((shards, halves, cap, LANES), f32),
            vmem((shards * cap, 2 * block), bf16),
            vmem((own, shards * cap), bf16),
            vmem((own, LANES), f32),
            vmem((gk, own), bf16),
            vmem((own, 2 * gk), bf16),
            vmem((own, 2 * block), bf16),
            vmem((gk, block), f32),
            vmem((2, gk, block), f32),
            vmem((2 * gk, 2 * block), bf16),
            vmem((rows, width_in), f32),
            vmem((rows, width_in), f32),
            vmem((rows, width_in), f32),
            vmem((shards, shards, cap), i32),
            vmem((silos, 1, gk), i32),
            pltpu.SMEM((shards, cap), i32),
            pltpu.SMEM((shards, shards), i32),
            pltpu.SMEM((1, silos), i32),
            pltpu.SemaphoreType.DMA((16,)),
            pltpu.SemaphoreType.DMA((shards,)),
            pltpu.SemaphoreType.DMA((shards,)),
            pltpu.SemaphoreType.DMA((2,)),
            pltpu.SemaphoreType.DMA((2,)),
        ],
        compiler_params=pltpu.CompilerParams(
            collective_id=0, has_side_effects=True, vmem_limit_bytes=24 << 20
        ),
    )(*operands)
    return (
        outs[0].reshape(params.shape),
        outs[1].reshape(estimate.shape),
        outs[2].reshape(mixed.shape),
        outs[3].reshape(error_memory.shape),
    )


def solution(mesh):
    in_specs = (
        P(("silo", "shard"), None),
        P(("silo", "shard"), None),
        P("silo", "shard", None, None),
        P("silo", "shard", None),
        P("silo", "shard", None),
        P("silo", "shard", None),
        P("silo", None, None, None),
        P("silo", None, None),
        P(None, "shard", None),
        P(None, "shard"),
    )
    out_specs = (
        P("silo", "shard", None),
        P("silo", "shard", None),
        P("silo", "shard", None),
        P("silo", "shard", None, None),
    )
    return jax.shard_map(body, mesh=mesh, in_specs=in_specs, out_specs=out_specs, check_vma=False)
```

```python
import functools

import jax
import jax.numpy as jnp
from jax import lax
from jax.experimental import pallas as pl
from jax.experimental.pallas import tpu as pltpu
from jax.sharding import PartitionSpec as P

LEARN_RATE = 0.25
CONSENSUS = 0.5
MIX_WEIGHT = 1.0 / 3.0
MESH = pl.DeviceIdType.MESH
LANES = 128


def split_pair(value):
    high = value.astype(jnp.bfloat16)
    low = (value - high.astype(jnp.float32)).astype(jnp.bfloat16)
    return high, low


def remote(src, dst, send, recv, target):
    return pltpu.make_async_remote_copy(
        src_ref=src, dst_ref=dst, send_sem=send, recv_sem=recv,
        device_id=target, device_id_type=MESH,
    )


def kernel(
    dims,
    activ_h, cot_h, mem_h, params_h, est_h, mixed_h, kept_h, kcnt_h, gos_h, gcnt_h,
    params_o, est_o, mixed_o, error_o,
    act_a, act_b, cot_v, cot_t, pend_a, pend_b, slots, arrived, pieces, onehot, mask_own, gos_take, gos_put,
    drift_p, gos_send, gos_recv, gos_p, par_v, est_v, mix_v, kept_v, gos_v,
    kept_s, kcnt_s, gcnt_s,
    load_sem, send_sem, recv_sem, gsend_sem, grecv_sem,
):
    silos, shards, own, cap, gk, tiles, block = dims
    rows = own // tiles
    act_v, pend = (act_a, act_b), (pend_a, pend_b)
    halves = len(pend)
    all_rows = rows * shards
    silo = lax.axis_index("silo")
    shard = lax.axis_index("shard")
    upper = lax.rem(silo + 1, silos)
    lower = lax.rem(silo + silos - 1, silos)
    scale = float(activ_h.shape[1]) ** -0.5
    count = [0]

    def load(src, dst):
        copy = pltpu.make_async_copy(src, dst, load_sem.at[count[0]])
        count[0] += 1
        copy.start()
        return copy

    def lanes_of(c, h):
        return pl.ds(c * block + h * LANES, LANES)

    def load_half(h):
        return [
            load(activ_h.at[:, lanes_of(c, h)], act_v[h].at[:, pl.ds(c * LANES, LANES)])
            for c in range(tiles)
        ]

    load_cot = load(cot_h, cot_v)
    load_kept_s = load(kept_h.at[shard], kept_s)
    load_act = [load_half(0)]

    barrier = pltpu.get_barrier_semaphore()
    for step in range(1, shards):
        pl.semaphore_signal(
            barrier, inc=1, device_id=(silo, lax.rem(shard + step, shards)), device_id_type=MESH
        )
    for other in (lower, upper):
        pl.semaphore_signal(barrier, inc=1, device_id=(other, shard), device_id_type=MESH)

    load_cot.wait()
    load_mem = []
    for h in range(halves):
        load_mem.append(load(mem_h.at[:, pl.ds(h * LANES, LANES)], pend[h]))
        if h + 1 < halves:
            load_act.append(load_half(h + 1))
    load_rest = [
        load(kept_h, kept_v),
        load(kcnt_h, kcnt_s),
        load(gos_h, gos_v),
        load(gcnt_h, gcnt_s),
        load(params_h, par_v),
        load(est_h, est_v),
        load(mixed_h, mix_v),
    ]
    cot_t[...] = cot_v[...].T

    def multiply(h):
        for copy in load_act[h]:
            copy.wait()
        for first in range(0, tiles, 2):
            these = range(first, min(first + 2, tiles))
            right = act_v[h][:, pl.ds(first * LANES, len(these) * LANES)]
            grad = jnp.dot(cot_t[...], right, preferred_element_type=jnp.float32) * scale
            if first == 0:
                load_mem[h].wait()
            for j, c in enumerate(these):
                view = pl.ds(c, all_rows, stride=tiles)
                pend[h][view, :] = pend[h][view, :] + grad[:, j * LANES : (j + 1) * LANES]

    def gather(owner, h):
        base = pl.multiple_of(owner * own, 8)

        def take(step, carry):
            first = pl.multiple_of(step * 8, 8)
            for j in range(8):
                row = base + kept_s[owner, first + j]
                slots[h, owner, pl.ds(first + j, 1), :] = pend[h][pl.ds(row, 1), :]
            return carry

        lax.fori_loop(0, cap // 8, take, 0)

    pairs = shards // 2
    sends = []
    for h in range(halves):
        multiply(h)
        if h == 0:
            load_kept_s.wait()
        if h == 0:
            pl.semaphore_wait(barrier, shards + 1)
        sends.append([])
        for far, side in ((2, 1), (1, 0), (3, 0), (1, 1), (3, 1), (2, 0), (0, 1), (0, 0)):
            owner = 2 * lax.rem(lax.div(shard, 2) + far, pairs) + lax.rem(shard + side, 2)
            gather(owner, h)
            step = 2 * far + side
            if step:
                copy = remote(
                    slots.at[h, owner], arrived.at[h, shard], send_sem.at[h, step],
                    recv_sem.at[h, step], (silo, owner),
                )
                copy.start()
                sends[h].append(copy)
            else:
                arrived[h, shard] = slots[h, shard]

    for copy in load_rest:
        copy.wait()

    lane_cap = lax.broadcasted_iota(jnp.int32, (1, cap), 1)
    lane_gk = lax.broadcasted_iota(jnp.int32, (1, gk), 1)

    order = lax.broadcasted_iota(jnp.int32, (own, 1), 0)
    block_of = lax.rem(order, rows) * tiles + lax.div(order, rows)
    for pair in range(shards // 2):
        ids = []
        for source in (2 * pair, 2 * pair + 1):
            filled = lane_cap < kcnt_s[source, shard]
            ids.append(jnp.where(filled, kept_v[source, pl.ds(shard, 1), :], -1))
        ids = jnp.concatenate(ids, axis=1)
        onehot[:, pl.ds(pair * 2 * cap, 2 * cap)] = jnp.where(block_of == ids, 1.0, 0.0).astype(
            jnp.bfloat16
        )

    def gossip_hot(which):
        ids = jnp.where(lane_gk < gcnt_s[0, which], gos_v[which], -1)
        return jnp.where(block_of == ids, 1.0, 0.0)

    mine = gossip_hot(silo)
    ones = jnp.ones((gk, LANES), jnp.bfloat16)
    mask_own[...] = jnp.dot(mine.astype(jnp.bfloat16), ones, preferred_element_type=jnp.float32)
    gos_take[...] = mine.T.astype(jnp.bfloat16)
    gos_put[:, pl.ds(0, gk)] = gossip_hot(lower).astype(jnp.bfloat16)
    gos_put[:, pl.ds(gk, gk)] = gossip_hot(upper).astype(jnp.bfloat16)

    goes = []

    def settle(h):
        for copy in sends[h]:
            copy.wait_recv()
        high, low = split_pair(arrived[h].reshape(shards * cap, LANES))
        pieces[h, :, pl.ds(0, LANES)] = high
        pieces[h, :, pl.ds(LANES, LANES)] = low
        added = jnp.dot(onehot[...], pieces[h], preferred_element_type=jnp.float32)
        added = added[:, :LANES] + added[:, LANES:]
        for c in range(tiles):
            part = pl.ds(c * rows, rows)
            cols = lanes_of(c, h)
            half = par_v[:, cols] - LEARN_RATE * added[c * rows : (c + 1) * rows]
            drift = half - est_v[:, cols]
            high, low = split_pair(drift)
            drift_p[h, part, pl.ds(0, LANES)] = high
            drift_p[h, part, pl.ds(LANES, LANES)] = low
            delta = jnp.where(mask_own[part, :] > 0.0, drift, 0.0)
            estimate = est_v[:, cols] + delta
            est_o[:, cols] = estimate
            mix_v[:, cols] = mix_v[:, cols] + MIX_WEIGHT * delta
            par_v[:, cols] = half - CONSENSUS * estimate
        taken = jnp.dot(gos_take[...], drift_p[h], preferred_element_type=jnp.float32)
        gos_send[h] = taken[:, :LANES] + taken[:, LANES:]
        for place, target in ((0, upper), (1, lower)):
            copy = remote(
                gos_send.at[h], gos_recv.at[h, place], gsend_sem.at[h, place],
                grecv_sem.at[h, place], (target, shard),
            )
            copy.start()
            goes.append(copy)

    def close(h):
        for copy in goes[2 * h : 2 * h + 2]:
            copy.wait_recv()
        high, low = split_pair(gos_recv[h].reshape(2 * gk, LANES))
        gos_p[h, :, pl.ds(0, LANES)] = high
        gos_p[h, :, pl.ds(LANES, LANES)] = low
        near = jnp.dot(gos_put[...], gos_p[h], preferred_element_type=jnp.float32)
        near = near[:, :LANES] + near[:, LANES:]
        for c in range(tiles):
            cols = lanes_of(c, h)
            mixed = mix_v[:, cols] + MIX_WEIGHT * near[c * rows : (c + 1) * rows]
            mixed_o[:, cols] = mixed
            params_o[:, cols] = par_v[:, cols] + CONSENSUS * mixed

    ones_cap = jnp.ones((cap, LANES), jnp.bfloat16)
    place_of = lax.broadcasted_iota(jnp.int32, (own, 1), 0)

    def clear(owner, carry):
        ids = jnp.where(lane_cap < kcnt_s[shard, owner], kept_v[shard, pl.ds(owner, 1), :], -1)
        hit = jnp.where(place_of == ids, 1.0, 0.0).astype(jnp.bfloat16)
        kept = jnp.dot(hit, ones_cap, preferred_element_type=jnp.float32)
        base = pl.multiple_of(owner * own, 8)
        for h in range(halves):
            error_o[pl.ds(base, own), pl.ds(h * LANES, LANES)] = jnp.where(
                kept > 0.0, 0.0, pend[h][pl.ds(base, own), :]
            )
        return carry

    settle(0)
    lax.fori_loop(0, shards, clear, 0)
    for h in range(1, halves):
        settle(h)
    for h in range(halves):
        close(h)
    for copy in [copy for group in sends for copy in group] + goes:
        copy.wait_send()


def finish(*refs):
    count = len(refs) // 2
    sems = refs[-1]
    copies = [
        pltpu.make_async_copy(refs[i], refs[count + i], sems.at[i]) for i in range(count)
    ]
    for copy in copies:
        copy.start()
    for copy in copies:
        copy.wait()


def body(
    activ, cotangent, error_memory, params, estimate, mixed,
    kept_blocks, kept_counts, gossip_blocks, gossip_counts,
):
    silos, shards = lax.axis_size("silo"), lax.axis_size("shard")
    tokens, width_in = activ.shape
    width_out = cotangent.shape[1]
    nblocks, block = error_memory.shape[2:]
    own = nblocks // shards
    cap, gk = kept_blocks.shape[3], gossip_blocks.shape[2]
    tiles = width_in // block
    halves = 2
    assert block == halves * LANES
    rows = own // tiles
    f32, bf16, i32 = jnp.float32, jnp.bfloat16, jnp.int32
    dims = (silos, shards, own, cap, gk, tiles, block)
    operands = (
        activ, cotangent, error_memory[0, 0], params[0], estimate[0], mixed[0],
        kept_blocks[0], kept_counts[0], gossip_blocks, gossip_counts.reshape(1, silos),
    )
    operands = tuple(pltpu.with_memory_space_constraint(x, pltpu.HBM) for x in operands)
    vmem = pltpu.VMEM
    outs = pl.pallas_call(
        functools.partial(kernel, dims),
        out_shape=(
            vmem((rows, width_in), f32),
            vmem((rows, width_in), f32),
            vmem((rows, width_in), f32),
            vmem((nblocks, block), f32),
        ),
        in_specs=[pl.BlockSpec(memory_space=pltpu.HBM)] * len(operands),
        out_specs=tuple([pl.BlockSpec(memory_space=pltpu.VMEM)] * 4),
        scratch_shapes=[
            vmem((tokens, tiles * LANES), bf16),
            vmem((tokens, tiles * LANES), bf16),
            vmem((tokens, width_out), bf16),
            vmem((width_out, tokens), bf16),
            vmem((nblocks, LANES), f32),
            vmem((nblocks, LANES), f32),
            vmem((halves, shards, cap, LANES), f32),
            vmem((halves, shards, cap, LANES), f32),
            vmem((halves, shards * cap, 2 * LANES), bf16),
            vmem((own, shards * cap), bf16),
            vmem((own, LANES), f32),
            vmem((gk, own), bf16),
            vmem((own, 2 * gk), bf16),
            vmem((halves, own, 2 * LANES), bf16),
            vmem((halves, gk, LANES), f32),
            vmem((halves, 2, gk, LANES), f32),
            vmem((halves, 2 * gk, 2 * LANES), bf16),
            vmem((rows, width_in), f32),
            vmem((rows, width_in), f32),
            vmem((rows, width_in), f32),
            vmem((shards, shards, cap), i32),
            vmem((silos, 1, gk), i32),
            pltpu.SMEM((shards, cap), i32),
            pltpu.SMEM((shards, shards), i32),
            pltpu.SMEM((1, silos), i32),
            pltpu.SemaphoreType.DMA((2 + halves * (tiles + 1) + 7,)),
            pltpu.SemaphoreType.DMA((halves, shards)),
            pltpu.SemaphoreType.DMA((halves, shards)),
            pltpu.SemaphoreType.DMA((halves, 2)),
            pltpu.SemaphoreType.DMA((halves, 2)),
        ],
        compiler_params=pltpu.CompilerParams(
            collective_id=0, has_side_effects=True, vmem_limit_bytes=24 << 20
        ),
    )(*operands)
    outs = pl.pallas_call(
        finish,
        out_shape=tuple(jax.ShapeDtypeStruct(x.shape, x.dtype) for x in outs),
        in_specs=[pl.BlockSpec(memory_space=pltpu.VMEM)] * len(outs),
        out_specs=tuple([pl.BlockSpec(memory_space=pltpu.HBM)] * len(outs)),
        scratch_shapes=[pltpu.SemaphoreType.DMA((len(outs),))],
        compiler_params=pltpu.CompilerParams(vmem_limit_bytes=1 << 20),
    )(*outs)
    return (
        outs[0].reshape(params.shape),
        outs[1].reshape(estimate.shape),
        outs[2].reshape(mixed.shape),
        outs[3].reshape(error_memory.shape),
    )


def solution(mesh):
    in_specs = (
        P(("silo", "shard"), None),
        P(("silo", "shard"), None),
        P("silo", "shard", None, None),
        P("silo", "shard", None),
        P("silo", "shard", None),
        P("silo", "shard", None),
        P("silo", None, None, None),
        P("silo", None, None),
        P(None, "shard", None),
        P(None, "shard"),
    )
    out_specs = (
        P("silo", "shard", None),
        P("silo", "shard", None),
        P("silo", "shard", None),
        P("silo", "shard", None, None),
    )
    return jax.shard_map(body, mesh=mesh, in_specs=in_specs, out_specs=out_specs, check_vma=False)
```

```python
import functools

import jax
import jax.numpy as jnp
from jax import lax
from jax.experimental import pallas as pl
from jax.experimental.pallas import tpu as pltpu
from jax.sharding import PartitionSpec as P

LEARN_RATE = 0.25
CONSENSUS = 0.5
MIX_WEIGHT = 1.0 / 3.0
MESH = pl.DeviceIdType.MESH
LANES = 128


def split_pair(value):
    high = value.astype(jnp.bfloat16)
    low = (value - high.astype(jnp.float32)).astype(jnp.bfloat16)
    return high, low


def remote(src, dst, send, recv, target):
    return pltpu.make_async_remote_copy(
        src_ref=src, dst_ref=dst, send_sem=send, recv_sem=recv,
        device_id=target, device_id_type=MESH,
    )


def kernel(
    dims,
    activ_h, cot_h, mem_h, params_h, est_h, mixed_h, kept_h, kcnt_h, gos_h, gcnt_h,
    params_o, est_o, mixed_o, error_o,
    act_a, act_b, cot_v, cot_t, pend_a, pend_b, slots, arrived, pieces, onehot, mask_own, gos_take, gos_put, gos_mix, gos_base,
    drift_p, gos_send, gos_recv, gos_p, par_v, est_v, mix_v, kept_v, gos_v,
    kept_s, kcnt_s, gcnt_s,
    load_sem, send_sem, recv_sem, gsend_sem, grecv_sem,
):
    silos, shards, own, cap, gk, tiles, block = dims
    rows = own // tiles
    act_v, pend = (act_a, act_b), (pend_a, pend_b)
    halves = len(pend)
    all_rows = rows * shards
    silo = lax.axis_index("silo")
    shard = lax.axis_index("shard")
    upper = lax.rem(silo + 1, silos)
    lower = lax.rem(silo + silos - 1, silos)
    scale = float(activ_h.shape[1]) ** -0.5
    count = [0]

    def load(src, dst):
        copy = pltpu.make_async_copy(src, dst, load_sem.at[count[0]])
        count[0] += 1
        copy.start()
        return copy

    def lanes_of(c, h):
        return pl.ds(c * block + h * LANES, LANES)

    def load_half(h):
        return [
            load(activ_h.at[:, lanes_of(c, h)], act_v[h].at[:, pl.ds(c * LANES, LANES)])
            for c in range(tiles)
        ]

    load_cot = load(cot_h, cot_v)
    load_act = [load_half(0)]
    load_kept_s = load(kept_h.at[shard], kept_s)
    load_mem = [load(mem_h.at[:, pl.ds(0, LANES)], pend[0])]

    barrier = pltpu.get_barrier_semaphore()
    for step in range(1, shards):
        pl.semaphore_signal(
            barrier, inc=1, device_id=(silo, lax.rem(shard + step, shards)), device_id_type=MESH
        )
    for other in (lower, upper):
        pl.semaphore_signal(barrier, inc=1, device_id=(other, shard), device_id_type=MESH)

    load_cot.wait()
    cot_t[...] = cot_v[...].T

    late = []

    def later():
        for h in range(1, halves):
            load_act.append(load_half(h))
            load_mem.append(load(mem_h.at[:, pl.ds(h * LANES, LANES)], pend[h]))
        return [
            load(kept_h, kept_v),
            load(kcnt_h, kcnt_s),
            load(gos_h, gos_v),
            load(gcnt_h, gcnt_s),
            load(params_h, par_v),
            load(est_h, est_v),
            load(mixed_h, mix_v),
        ]

    def multiply(h):
        for copy in load_act[h]:
            copy.wait()
        for first in range(0, tiles, 2):
            these = range(first, min(first + 2, tiles))
            right = act_v[h][:, pl.ds(first * LANES, len(these) * LANES)]
            grad = jnp.dot(cot_t[...], right, preferred_element_type=jnp.float32) * scale
            if first == 0:
                load_mem[h].wait()
                if h == 0:
                    late.extend(later())
            for j, c in enumerate(these):
                view = pl.ds(c, all_rows, stride=tiles)
                pend[h][view, :] = pend[h][view, :] + grad[:, j * LANES : (j + 1) * LANES]

    def gather(owner, h):
        blocks = pend[h].at[pl.ds(pl.multiple_of(owner * own, 8), own)]
        for k in range(cap):
            slots[h, owner, pl.ds(k, 1), :] = blocks[pl.ds(kept_s[owner, k], 1), :]

    pairs = shards // 2
    sends = []
    for h in range(halves):
        multiply(h)
        if h == 0:
            load_kept_s.wait()
        if h == 0:
            pl.semaphore_wait(barrier, shards + 1)
        sends.append([])
        for far, side in ((2, 1), (1, 0), (3, 0), (1, 1), (3, 1), (2, 0), (0, 1), (0, 0)):
            owner = 2 * lax.rem(lax.div(shard, 2) + far, pairs) + lax.rem(shard + side, 2)
            gather(owner, h)
            step = 2 * far + side
            if step:
                copy = remote(
                    slots.at[h, owner], arrived.at[h, shard], send_sem.at[h, step],
                    recv_sem.at[h, step], (silo, owner),
                )
                copy.start()
                sends[h].append(copy)
            else:
                arrived[h, shard] = slots[h, shard]

    for copy in late:
        copy.wait()

    lane_cap = lax.broadcasted_iota(jnp.int32, (1, cap), 1)
    lane_gk = lax.broadcasted_iota(jnp.int32, (1, gk), 1)

    order = lax.broadcasted_iota(jnp.int32, (own, 1), 0)
    block_of = lax.rem(order, rows) * tiles + lax.div(order, rows)
    for pair in range(shards // 2):
        ids = []
        for source in (2 * pair, 2 * pair + 1):
            filled = lane_cap < kcnt_s[source, shard]
            ids.append(jnp.where(filled, kept_v[source, pl.ds(shard, 1), :], -1))
        ids = jnp.concatenate(ids, axis=1)
        onehot[:, pl.ds(pair * 2 * cap, 2 * cap)] = jnp.where(block_of == ids, 1.0, 0.0).astype(
            jnp.bfloat16
        )

    def gossip_hot(which):
        ids = jnp.where(lane_gk < gcnt_s[0, which], gos_v[which], -1)
        return jnp.where(block_of == ids, 1.0, 0.0)

    mine = gossip_hot(silo)
    ones = jnp.ones((gk, LANES), jnp.bfloat16)
    mask_own[...] = jnp.dot(mine.astype(jnp.bfloat16), ones, preferred_element_type=jnp.float32)
    gos_take[...] = mine.T.astype(jnp.bfloat16)
    gos_put[:, pl.ds(0, gk)] = gossip_hot(lower).astype(jnp.bfloat16)
    gos_put[:, pl.ds(gk, gk)] = gossip_hot(upper).astype(jnp.bfloat16)

    gos_mix[...] = jnp.dot(
        gos_take[...], onehot[...], preferred_element_type=jnp.float32
    ).astype(jnp.bfloat16)
    for h in range(halves):
        for c in range(tiles):
            part = pl.ds(c * rows, rows)
            high, low = split_pair(par_v[:, lanes_of(c, h)] - est_v[:, lanes_of(c, h)])
            drift_p[part, pl.ds(0, LANES)] = high
            drift_p[part, pl.ds(LANES, LANES)] = low
        taken = jnp.dot(gos_take[...], drift_p[...], preferred_element_type=jnp.float32)
        gos_base[h] = taken[:, :LANES] + taken[:, LANES:]

    goes = []

    def settle(h):
        for copy in sends[h]:
            copy.wait_recv()
        high, low = split_pair(arrived[h].reshape(shards * cap, LANES))
        pieces[h, :, pl.ds(0, LANES)] = high
        pieces[h, :, pl.ds(LANES, LANES)] = low
        taken = jnp.dot(gos_mix[...], pieces[h], preferred_element_type=jnp.float32)
        gos_send[h] = gos_base[h] - LEARN_RATE * (taken[:, :LANES] + taken[:, LANES:])
        for place, target in ((0, upper), (1, lower)):
            copy = remote(
                gos_send.at[h], gos_recv.at[h, place], gsend_sem.at[h, place],
                grecv_sem.at[h, place], (target, shard),
            )
            copy.start()
            goes.append(copy)

    def update(h):
        added = jnp.dot(onehot[...], pieces[h], preferred_element_type=jnp.float32)
        added = added[:, :LANES] + added[:, LANES:]
        for c in range(tiles):
            part = pl.ds(c * rows, rows)
            cols = lanes_of(c, h)
            half = par_v[:, cols] - LEARN_RATE * added[c * rows : (c + 1) * rows]
            delta = jnp.where(mask_own[part, :] > 0.0, half - est_v[:, cols], 0.0)
            estimate = est_v[:, cols] + delta
            est_o[:, cols] = estimate
            mix_v[:, cols] = mix_v[:, cols] + MIX_WEIGHT * delta
            par_v[:, cols] = half - CONSENSUS * estimate

    def close(h):
        for copy in goes[2 * h : 2 * h + 2]:
            copy.wait_recv()
        high, low = split_pair(gos_recv[h].reshape(2 * gk, LANES))
        gos_p[h, :, pl.ds(0, LANES)] = high
        gos_p[h, :, pl.ds(LANES, LANES)] = low
        near = jnp.dot(gos_put[...], gos_p[h], preferred_element_type=jnp.float32)
        near = near[:, :LANES] + near[:, LANES:]
        for c in range(tiles):
            cols = lanes_of(c, h)
            mixed = mix_v[:, cols] + MIX_WEIGHT * near[c * rows : (c + 1) * rows]
            mixed_o[:, cols] = mixed
            params_o[:, cols] = par_v[:, cols] + CONSENSUS * mixed

    ones_cap = jnp.ones((cap, LANES), jnp.bfloat16)
    place_of = lax.broadcasted_iota(jnp.int32, (own, 1), 0)

    def clear(owner, carry):
        ids = jnp.where(lane_cap < kcnt_s[shard, owner], kept_v[shard, pl.ds(owner, 1), :], -1)
        hit = jnp.where(place_of == ids, 1.0, 0.0).astype(jnp.bfloat16)
        kept = jnp.dot(hit, ones_cap, preferred_element_type=jnp.float32)
        base = pl.multiple_of(owner * own, 8)
        for h in range(halves):
            error_o[pl.ds(base, own), pl.ds(h * LANES, LANES)] = jnp.where(
                kept > 0.0, 0.0, pend[h][pl.ds(base, own), :]
            )
        return carry

    lax.fori_loop(0, shards, clear, 0)
    for h in range(halves):
        settle(h)
        update(h)
    for h in range(halves):
        close(h)
    for copy in [copy for group in sends for copy in group] + goes:
        copy.wait_send()


def finish(*refs):
    count = len(refs) // 2
    sems = refs[-1]
    copies = [
        pltpu.make_async_copy(refs[i], refs[count + i], sems.at[i]) for i in range(count)
    ]
    for copy in copies:
        copy.start()
    for copy in copies:
        copy.wait()


def body(
    activ, cotangent, error_memory, params, estimate, mixed,
    kept_blocks, kept_counts, gossip_blocks, gossip_counts,
):
    silos, shards = lax.axis_size("silo"), lax.axis_size("shard")
    tokens, width_in = activ.shape
    width_out = cotangent.shape[1]
    nblocks, block = error_memory.shape[2:]
    own = nblocks // shards
    cap, gk = kept_blocks.shape[3], gossip_blocks.shape[2]
    tiles = width_in // block
    halves = 2
    assert block == halves * LANES
    rows = own // tiles
    f32, bf16, i32 = jnp.float32, jnp.bfloat16, jnp.int32
    dims = (silos, shards, own, cap, gk, tiles, block)
    operands = (
        activ, cotangent, error_memory[0, 0], params[0], estimate[0], mixed[0],
        kept_blocks[0], kept_counts[0], gossip_blocks, gossip_counts.reshape(1, silos),
    )
    operands = tuple(pltpu.with_memory_space_constraint(x, pltpu.HBM) for x in operands)
    vmem = pltpu.VMEM
    outs = pl.pallas_call(
        functools.partial(kernel, dims),
        out_shape=(
            vmem((rows, width_in), f32),
            vmem((rows, width_in), f32),
            vmem((rows, width_in), f32),
            vmem((nblocks, block), f32),
        ),
        in_specs=[pl.BlockSpec(memory_space=pltpu.HBM)] * len(operands),
        out_specs=tuple([pl.BlockSpec(memory_space=pltpu.VMEM)] * 4),
        scratch_shapes=[
            vmem((tokens, tiles * LANES), bf16),
            vmem((tokens, tiles * LANES), bf16),
            vmem((tokens, width_out), bf16),
            vmem((width_out, tokens), bf16),
            vmem((nblocks, LANES), f32),
            vmem((nblocks, LANES), f32),
            vmem((halves, shards, cap, LANES), f32),
            vmem((halves, shards, cap, LANES), f32),
            vmem((halves, shards * cap, 2 * LANES), bf16),
            vmem((own, shards * cap), bf16),
            vmem((own, LANES), f32),
            vmem((gk, own), bf16),
            vmem((own, 2 * gk), bf16),
            vmem((gk, shards * cap), bf16),
            vmem((halves, gk, LANES), f32),
            vmem((own, 2 * LANES), bf16),
            vmem((halves, gk, LANES), f32),
            vmem((halves, 2, gk, LANES), f32),
            vmem((halves, 2 * gk, 2 * LANES), bf16),
            vmem((rows, width_in), f32),
            vmem((rows, width_in), f32),
            vmem((rows, width_in), f32),
            vmem((shards, shards, cap), i32),
            vmem((silos, 1, gk), i32),
            pltpu.SMEM((shards, cap), i32),
            pltpu.SMEM((shards, shards), i32),
            pltpu.SMEM((1, silos), i32),
            pltpu.SemaphoreType.DMA((2 + halves * (tiles + 1) + 7,)),
            pltpu.SemaphoreType.DMA((halves, shards)),
            pltpu.SemaphoreType.DMA((halves, shards)),
            pltpu.SemaphoreType.DMA((halves, 2)),
            pltpu.SemaphoreType.DMA((halves, 2)),
        ],
        compiler_params=pltpu.CompilerParams(
            collective_id=0, has_side_effects=True, vmem_limit_bytes=24 << 20
        ),
    )(*operands)
    outs = pl.pallas_call(
        finish,
        out_shape=tuple(jax.ShapeDtypeStruct(x.shape, x.dtype) for x in outs),
        in_specs=[pl.BlockSpec(memory_space=pltpu.VMEM)] * len(outs),
        out_specs=tuple([pl.BlockSpec(memory_space=pltpu.HBM)] * len(outs)),
        scratch_shapes=[pltpu.SemaphoreType.DMA((len(outs),))],
        compiler_params=pltpu.CompilerParams(vmem_limit_bytes=1 << 20),
    )(*outs)
    return (
        outs[0].reshape(params.shape),
        outs[1].reshape(estimate.shape),
        outs[2].reshape(mixed.shape),
        outs[3].reshape(error_memory.shape),
    )


def solution(mesh):
    in_specs = (
        P(("silo", "shard"), None),
        P(("silo", "shard"), None),
        P("silo", "shard", None, None),
        P("silo", "shard", None),
        P("silo", "shard", None),
        P("silo", "shard", None),
        P("silo", None, None, None),
        P("silo", None, None),
        P(None, "shard", None),
        P(None, "shard"),
    )
    out_specs = (
        P("silo", "shard", None),
        P("silo", "shard", None),
        P("silo", "shard", None),
        P("silo", "shard", None, None),
    )
    return jax.shard_map(body, mesh=mesh, in_specs=in_specs, out_specs=out_specs, check_vma=False)
```

```python
import functools

import jax
import jax.numpy as jnp
from jax import lax
from jax.experimental import pallas as pl
from jax.experimental.pallas import tpu as pltpu
from jax.sharding import PartitionSpec as P

LEARN_RATE = 0.25
CONSENSUS = 0.5
MIX_WEIGHT = 1.0 / 3.0
MESH = pl.DeviceIdType.MESH
LANES = 128


def split_pair(value):
    high = value.astype(jnp.bfloat16)
    low = (value - high.astype(jnp.float32)).astype(jnp.bfloat16)
    return high, low


def remote(src, dst, send, recv, target):
    return pltpu.make_async_remote_copy(
        src_ref=src, dst_ref=dst, send_sem=send, recv_sem=recv,
        device_id=target, device_id_type=MESH,
    )


def kernel(
    dims,
    activ_h, cot_h, mem_h, params_h, est_h, mixed_h, kept_h, kcnt_h, gos_h, gcnt_h,
    params_o, est_o, mixed_o, error_o,
    act_a, act_b, cot_v, cot_t, pend_a, pend_b, slots, arrived, pieces, onehot, mask_own, gos_take, gos_put, gos_mix, gos_base,
    drift_p, gos_send, gos_recv, gos_p, par_v, est_v, mix_v, kept_v, gos_v,
    kept_s, kcnt_s, gcnt_s,
    load_sem, send_sem, recv_sem, gsend_sem, grecv_sem, near_sem,
):
    silos, shards, own, cap, gk, tiles, block = dims
    rows = own // tiles
    act_v, pend = (act_a, act_b), (pend_a, pend_b)
    halves = len(pend)
    all_rows = rows * shards
    silo = lax.axis_index("silo")
    shard = lax.axis_index("shard")
    upper = lax.rem(silo + 1, silos)
    lower = lax.rem(silo + silos - 1, silos)
    scale = float(activ_h.shape[1]) ** -0.5
    count = [0]

    def load(src, dst):
        copy = pltpu.make_async_copy(src, dst, load_sem.at[count[0]])
        count[0] += 1
        copy.start()
        return copy

    def lanes_of(c, h):
        return pl.ds(c * block + h * LANES, LANES)

    def load_half(h):
        return [
            load(activ_h.at[:, lanes_of(c, h)], act_v[h].at[:, pl.ds(c * LANES, LANES)])
            for c in range(tiles)
        ]

    load_cot = load(cot_h, cot_v)
    load_act = [load_half(0)]
    load_kept_s = load(kept_h.at[shard], kept_s)
    load_mem = [load(mem_h.at[:, pl.ds(0, LANES)], pend[0])]

    barrier = pltpu.get_barrier_semaphore()
    for step in range(1, shards):
        pl.semaphore_signal(
            barrier, inc=1, device_id=(silo, lax.rem(shard + step, shards)), device_id_type=MESH
        )
    last = silos - 1

    @pl.when(silo != last)
    def _():
        pl.semaphore_signal(barrier, inc=1, device_id=(upper, shard), device_id_type=MESH)

    @pl.when(silo == 0)
    def _():
        pl.semaphore_signal(barrier, inc=1, device_id=(lower, shard), device_id_type=MESH)

    def enter():
        greeted = jnp.where(silo == 0, 0, jnp.where(silo == last, 2, 1))
        pl.semaphore_wait(barrier, shards - 1 + greeted)

        @pl.when(silo != 0)
        def _():
            pl.semaphore_signal(near_sem, inc=1, device_id=(lower, shard), device_id_type=MESH)

        @pl.when(silo == last)
        def _():
            pl.semaphore_signal(near_sem, inc=1, device_id=(upper, shard), device_id_type=MESH)

    def await_near():
        @pl.when(silo != last)
        def _():
            pl.semaphore_wait(near_sem, jnp.where(silo == 0, 2, 1))

    load_cot.wait()
    pairs = shards // 2
    here, side = lax.div(shard, 2), lax.rem(shard, 2)

    def owner_at(turn):
        far = (turn + 1) % pairs
        return 2 * lax.rem(here + far, pairs) + (1 - side if turn < pairs else side)

    turned = cot_v[...].T
    for owner in range(shards):
        turn = lax.rem(owner // 2 - here + 2 * pairs - 1, pairs) + jnp.where(
            side == owner % 2, pairs, 0
        )
        cot_t[pl.ds(pl.multiple_of(turn * rows, 16), rows), :] = turned[
            owner * rows : (owner + 1) * rows
        ]

    late = []

    def later():
        for h in range(1, halves):
            load_act.append(load_half(h))
            load_mem.append(load(mem_h.at[:, pl.ds(h * LANES, LANES)], pend[h]))
        return [
            load(kept_h, kept_v),
            load(kcnt_h, kcnt_s),
            load(gos_h, gos_v),
            load(gcnt_h, gcnt_s),
            load(params_h, par_v),
            load(est_h, est_v),
            load(mixed_h, mix_v),
        ]

    def multiply(h, turns):
        if turns[0] == 0:
            for copy in load_act[h]:
                copy.wait()
        left = cot_t[turns[0] * rows : (turns[-1] + 1) * rows, :]
        for first in range(0, tiles, 2):
            these = range(first, min(first + 2, tiles))
            right = act_v[h][:, pl.ds(first * LANES, len(these) * LANES)]
            grad = jnp.dot(left, right, preferred_element_type=jnp.float32) * scale
            if first == 0 and turns[0] == 0:
                load_mem[h].wait()
                if h == 0:
                    late.extend(later())
            for place, turn in enumerate(turns):
                base = pl.multiple_of(owner_at(turn) * own, 8)
                for j, c in enumerate(these):
                    view = pl.ds(base + c, rows, stride=tiles)
                    pend[h][view, :] = (
                        pend[h][view, :]
                        + grad[place * rows : (place + 1) * rows, j * LANES : (j + 1) * LANES]
                    )

    def gather(owner, h):
        blocks = pend[h].at[pl.ds(pl.multiple_of(owner * own, 8), own)]
        for k in range(cap):
            slots[h, owner, pl.ds(k, 1), :] = blocks[pl.ds(kept_s[owner, k], 1), :]

    sends = []
    for h in range(halves):
        sends.append([])
        for turns in (range(pairs), range(pairs, shards)):
            multiply(h, turns)
            if h == 0 and turns[0] == 0:
                load_kept_s.wait()
                enter()
            for turn in turns:
                owner = owner_at(turn)
                gather(owner, h)
                if turn < shards - 1:
                    copy = remote(
                        slots.at[h, owner], arrived.at[h, shard], send_sem.at[h, turn],
                        recv_sem.at[h, turn], (silo, owner),
                    )
                    copy.start()
                    sends[h].append(copy)
                else:
                    arrived[h, shard] = slots[h, shard]

    for copy in late:
        copy.wait()

    lane_cap = lax.broadcasted_iota(jnp.int32, (1, cap), 1)
    lane_gk = lax.broadcasted_iota(jnp.int32, (1, gk), 1)

    order = lax.broadcasted_iota(jnp.int32, (own, 1), 0)
    block_of = lax.rem(order, rows) * tiles + lax.div(order, rows)
    for pair in range(shards // 2):
        ids = []
        for source in (2 * pair, 2 * pair + 1):
            filled = lane_cap < kcnt_s[source, shard]
            ids.append(jnp.where(filled, kept_v[source, pl.ds(shard, 1), :], -1))
        ids = jnp.concatenate(ids, axis=1)
        onehot[:, pl.ds(pair * 2 * cap, 2 * cap)] = jnp.where(block_of == ids, 1.0, 0.0).astype(
            jnp.bfloat16
        )

    def gossip_hot(which):
        ids = jnp.where(lane_gk < gcnt_s[0, which], gos_v[which], -1)
        return jnp.where(block_of == ids, 1.0, 0.0)

    mine = gossip_hot(silo)
    ones = jnp.ones((gk, LANES), jnp.bfloat16)
    mask_own[...] = jnp.dot(mine.astype(jnp.bfloat16), ones, preferred_element_type=jnp.float32)
    gos_take[...] = mine.T.astype(jnp.bfloat16)
    gos_put[:, pl.ds(0, gk)] = gossip_hot(lower).astype(jnp.bfloat16)
    gos_put[:, pl.ds(gk, gk)] = gossip_hot(upper).astype(jnp.bfloat16)

    gos_mix[...] = jnp.dot(
        gos_take[...], onehot[...], preferred_element_type=jnp.float32
    ).astype(jnp.bfloat16)
    for h in range(halves):
        for c in range(tiles):
            part = pl.ds(c * rows, rows)
            high, low = split_pair(par_v[:, lanes_of(c, h)] - est_v[:, lanes_of(c, h)])
            drift_p[part, pl.ds(0, LANES)] = high
            drift_p[part, pl.ds(LANES, LANES)] = low
        taken = jnp.dot(gos_take[...], drift_p[...], preferred_element_type=jnp.float32)
        gos_base[h] = taken[:, :LANES] + taken[:, LANES:]

    goes = []

    def settle(h):
        for copy in sends[h]:
            copy.wait_recv()
        high, low = split_pair(arrived[h].reshape(shards * cap, LANES))
        pieces[h, :, pl.ds(0, LANES)] = high
        pieces[h, :, pl.ds(LANES, LANES)] = low
        taken = jnp.dot(gos_mix[...], pieces[h], preferred_element_type=jnp.float32)
        gos_send[h] = gos_base[h] - LEARN_RATE * (taken[:, :LANES] + taken[:, LANES:])
        for place, target in ((0, upper), (1, lower)):
            copy = remote(
                gos_send.at[h], gos_recv.at[h, place], gsend_sem.at[h, place],
                grecv_sem.at[h, place], (target, shard),
            )
            copy.start()
            goes.append(copy)

    def update(h):
        added = jnp.dot(onehot[...], pieces[h], preferred_element_type=jnp.float32)
        added = added[:, :LANES] + added[:, LANES:]
        for c in range(tiles):
            part = pl.ds(c * rows, rows)
            cols = lanes_of(c, h)
            half = par_v[:, cols] - LEARN_RATE * added[c * rows : (c + 1) * rows]
            delta = jnp.where(mask_own[part, :] > 0.0, half - est_v[:, cols], 0.0)
            estimate = est_v[:, cols] + delta
            est_o[:, cols] = estimate
            mix_v[:, cols] = mix_v[:, cols] + MIX_WEIGHT * delta
            par_v[:, cols] = half - CONSENSUS * estimate

    def close(h):
        for copy in goes[2 * h : 2 * h + 2]:
            copy.wait_recv()
        high, low = split_pair(gos_recv[h].reshape(2 * gk, LANES))
        gos_p[h, :, pl.ds(0, LANES)] = high
        gos_p[h, :, pl.ds(LANES, LANES)] = low
        near = jnp.dot(gos_put[...], gos_p[h], preferred_element_type=jnp.float32)
        near = near[:, :LANES] + near[:, LANES:]
        for c in range(tiles):
            cols = lanes_of(c, h)
            mixed = mix_v[:, cols] + MIX_WEIGHT * near[c * rows : (c + 1) * rows]
            mixed_o[:, cols] = mixed
            params_o[:, cols] = par_v[:, cols] + CONSENSUS * mixed

    ones_cap = jnp.ones((cap, LANES), jnp.bfloat16)
    place_of = lax.broadcasted_iota(jnp.int32, (own, 1), 0)

    def clear(owner, carry):
        ids = jnp.where(lane_cap < kcnt_s[shard, owner], kept_v[shard, pl.ds(owner, 1), :], -1)
        hit = jnp.where(place_of == ids, 1.0, 0.0).astype(jnp.bfloat16)
        kept = jnp.dot(hit, ones_cap, preferred_element_type=jnp.float32)
        base = pl.multiple_of(owner * own, 8)
        for h in range(halves):
            error_o[pl.ds(base, own), pl.ds(h * LANES, LANES)] = jnp.where(
                kept > 0.0, 0.0, pend[h][pl.ds(base, own), :]
            )
        return carry

    lax.fori_loop(0, shards, clear, 0)
    await_near()
    for h in range(halves):
        settle(h)
        update(h)
    for h in range(halves):
        close(h)
    for copy in [copy for group in sends for copy in group] + goes:
        copy.wait_send()


def finish(*refs):
    count = len(refs) // 2
    sems = refs[-1]
    copies = [
        pltpu.make_async_copy(refs[i], refs[count + i], sems.at[i]) for i in range(count)
    ]
    for copy in copies:
        copy.start()
    for copy in copies:
        copy.wait()


def body(
    activ, cotangent, error_memory, params, estimate, mixed,
    kept_blocks, kept_counts, gossip_blocks, gossip_counts,
):
    silos, shards = lax.axis_size("silo"), lax.axis_size("shard")
    tokens, width_in = activ.shape
    width_out = cotangent.shape[1]
    nblocks, block = error_memory.shape[2:]
    own = nblocks // shards
    cap, gk = kept_blocks.shape[3], gossip_blocks.shape[2]
    tiles = width_in // block
    halves = 2
    assert block == halves * LANES
    rows = own // tiles
    f32, bf16, i32 = jnp.float32, jnp.bfloat16, jnp.int32
    dims = (silos, shards, own, cap, gk, tiles, block)
    operands = (
        activ, cotangent, error_memory[0, 0], params[0], estimate[0], mixed[0],
        kept_blocks[0], kept_counts[0], gossip_blocks, gossip_counts.reshape(1, silos),
    )
    operands = tuple(pltpu.with_memory_space_constraint(x, pltpu.HBM) for x in operands)
    vmem = pltpu.VMEM
    outs = pl.pallas_call(
        functools.partial(kernel, dims),
        out_shape=(
            vmem((rows, width_in), f32),
            vmem((rows, width_in), f32),
            vmem((rows, width_in), f32),
            vmem((nblocks, block), f32),
        ),
        in_specs=[pl.BlockSpec(memory_space=pltpu.HBM)] * len(operands),
        out_specs=tuple([pl.BlockSpec(memory_space=pltpu.VMEM)] * 4),
        scratch_shapes=[
            vmem((tokens, tiles * LANES), bf16),
            vmem((tokens, tiles * LANES), bf16),
            vmem((tokens, width_out), bf16),
            vmem((width_out, tokens), bf16),
            vmem((nblocks, LANES), f32),
            vmem((nblocks, LANES), f32),
            vmem((halves, shards, cap, LANES), f32),
            vmem((halves, shards, cap, LANES), f32),
            vmem((halves, shards * cap, 2 * LANES), bf16),
            vmem((own, shards * cap), bf16),
            vmem((own, LANES), f32),
            vmem((gk, own), bf16),
            vmem((own, 2 * gk), bf16),
            vmem((gk, shards * cap), bf16),
            vmem((halves, gk, LANES), f32),
            vmem((own, 2 * LANES), bf16),
            vmem((halves, gk, LANES), f32),
            vmem((halves, 2, gk, LANES), f32),
            vmem((halves, 2 * gk, 2 * LANES), bf16),
            vmem((rows, width_in), f32),
            vmem((rows, width_in), f32),
            vmem((rows, width_in), f32),
            vmem((shards, shards, cap), i32),
            vmem((silos, 1, gk), i32),
            pltpu.SMEM((shards, cap), i32),
            pltpu.SMEM((shards, shards), i32),
            pltpu.SMEM((1, silos), i32),
            pltpu.SemaphoreType.DMA((2 + halves * (tiles + 1) + 7,)),
            pltpu.SemaphoreType.DMA((halves, shards - 1)),
            pltpu.SemaphoreType.DMA((halves, shards - 1)),
            pltpu.SemaphoreType.DMA((halves, 2)),
            pltpu.SemaphoreType.DMA((halves, 2)),
            pltpu.SemaphoreType.REGULAR,
        ],
        compiler_params=pltpu.CompilerParams(
            collective_id=0, has_side_effects=True, vmem_limit_bytes=24 << 20
        ),
    )(*operands)
    outs = pl.pallas_call(
        finish,
        out_shape=tuple(jax.ShapeDtypeStruct(x.shape, x.dtype) for x in outs),
        in_specs=[pl.BlockSpec(memory_space=pltpu.VMEM)] * len(outs),
        out_specs=tuple([pl.BlockSpec(memory_space=pltpu.HBM)] * len(outs)),
        scratch_shapes=[pltpu.SemaphoreType.DMA((len(outs),))],
        compiler_params=pltpu.CompilerParams(vmem_limit_bytes=1 << 20),
    )(*outs)
    return (
        outs[0].reshape(params.shape),
        outs[1].reshape(estimate.shape),
        outs[2].reshape(mixed.shape),
        outs[3].reshape(error_memory.shape),
    )


def solution(mesh):
    in_specs = (
        P(("silo", "shard"), None),
        P(("silo", "shard"), None),
        P("silo", "shard", None, None),
        P("silo", "shard", None),
        P("silo", "shard", None),
        P("silo", "shard", None),
        P("silo", None, None, None),
        P("silo", None, None),
        P(None, "shard", None),
        P(None, "shard"),
    )
    out_specs = (
        P("silo", "shard", None),
        P("silo", "shard", None),
        P("silo", "shard", None),
        P("silo", "shard", None, None),
    )
    return jax.shard_map(body, mesh=mesh, in_specs=in_specs, out_specs=out_specs, check_vma=False)
```

```python
import functools

import jax
import jax.numpy as jnp
from jax import lax
from jax.experimental import pallas as pl
from jax.experimental.pallas import tpu as pltpu
from jax.sharding import PartitionSpec as P

LEARN_RATE = 0.25
CONSENSUS = 0.5
MIX_WEIGHT = 1.0 / 3.0
MESH = pl.DeviceIdType.MESH
LANES = 128


def split_pair(value):
    high = value.astype(jnp.bfloat16)
    low = (value - high.astype(jnp.float32)).astype(jnp.bfloat16)
    return high, low


def remote(src, dst, send, recv, target):
    return pltpu.make_async_remote_copy(
        src_ref=src, dst_ref=dst, send_sem=send, recv_sem=recv,
        device_id=target, device_id_type=MESH,
    )


def kernel(
    dims,
    activ_h, cot_h, mem_h, params_h, est_h, mixed_h, kept_h, kcnt_h, gos_h, gcnt_h,
    params_o, est_o, mixed_o, error_o,
    act_a, act_b, cot_v, cot_t, pend_a, pend_b, slots, arrived, pieces, onehot, mask_own, gos_take, gos_put, gos_mix, gos_base,
    drift_p, gos_send, gos_recv, gos_p, par_v, est_v, mix_v, kept_v, gos_v,
    kept_s, kcnt_s, gcnt_s,
    load_sem, send_sem, recv_sem, gsend_sem, grecv_sem, near_sem,
):
    silos, shards, own, cap, gk, tiles, block = dims
    rows = own // tiles
    act_v, pend = (act_a, act_b), (pend_a, pend_b)
    halves = len(pend)
    all_rows = rows * shards
    silo = lax.axis_index("silo")
    shard = lax.axis_index("shard")
    upper = lax.rem(silo + 1, silos)
    lower = lax.rem(silo + silos - 1, silos)
    scale = float(activ_h.shape[1]) ** -0.5
    pairs = shards // 2
    here, side = lax.div(shard, 2), lax.rem(shard, 2)

    def owner_at(turn):
        far = (turn + 1) % pairs
        return 2 * lax.rem(here + far, pairs) + (1 - side if turn < pairs else side)

    count = [0]

    def load(src, dst):
        copy = pltpu.make_async_copy(src, dst, load_sem.at[count[0]])
        count[0] += 1
        copy.start()
        return copy

    def lanes_of(c, h):
        return pl.ds(c * block + h * LANES, LANES)

    def load_all(copies, whole):
        sem = load_sem.at[count[0]]
        count[0] += 1
        for src, dst in copies:
            pltpu.make_async_copy(src, dst, sem).start()
        return pltpu.make_async_copy(whole[0], whole[1], sem)

    def load_half(h):
        return load_all(
            [
                (activ_h.at[:, lanes_of(c, h)], act_v[h].at[:, pl.ds(c * LANES, LANES)])
                for c in range(tiles)
            ],
            (activ_h.at[:, pl.ds(0, tiles * LANES)], act_v[h]),
        )

    def load_pend(h, turns):
        lanes = pl.ds(h * LANES, LANES)
        views = [pl.ds(pl.multiple_of(owner_at(turn) * own, 8), own) for turn in turns]
        whole = pl.ds(0, len(turns) * own)
        return load_all(
            [(mem_h.at[view, lanes], pend[h].at[view]) for view in views],
            (mem_h.at[whole, lanes], pend[h].at[whole]),
        )

    parts = (range(pairs), range(pairs, shards))
    load_cot = load(cot_h, cot_v)
    load_act = [load_half(0)]
    load_kept_s = load(kept_h.at[shard], kept_s)
    load_mem = [[load_pend(0, turns) for turns in parts]]

    barrier = pltpu.get_barrier_semaphore()
    for step in range(1, shards):
        pl.semaphore_signal(
            barrier, inc=1, device_id=(silo, lax.rem(shard + step, shards)), device_id_type=MESH
        )
    last = silos - 1

    @pl.when(silo != last)
    def _():
        pl.semaphore_signal(barrier, inc=1, device_id=(upper, shard), device_id_type=MESH)

    @pl.when(silo == 0)
    def _():
        pl.semaphore_signal(barrier, inc=1, device_id=(lower, shard), device_id_type=MESH)

    def enter():
        greeted = jnp.where(silo == 0, 0, jnp.where(silo == last, 2, 1))
        pl.semaphore_wait(barrier, shards - 1 + greeted)

        @pl.when(silo != 0)
        def _():
            pl.semaphore_signal(near_sem, inc=1, device_id=(lower, shard), device_id_type=MESH)

        @pl.when(silo == last)
        def _():
            pl.semaphore_signal(near_sem, inc=1, device_id=(upper, shard), device_id_type=MESH)

    def await_near():
        @pl.when(silo != last)
        def _():
            pl.semaphore_wait(near_sem, jnp.where(silo == 0, 2, 1))

    load_cot.wait()
    turned = cot_v[...].T
    for owner in range(shards):
        turn = lax.rem(owner // 2 - here + 2 * pairs - 1, pairs) + jnp.where(
            side == owner % 2, pairs, 0
        )
        cot_t[pl.ds(pl.multiple_of(turn * rows, 16), rows), :] = turned[
            owner * rows : (owner + 1) * rows
        ]

    late = []

    def later():
        for h in range(1, halves):
            load_act.append(load_half(h))
            load_mem.append([load_pend(h, turns) for turns in parts])
        return [
            load(kept_h, kept_v),
            load(kcnt_h, kcnt_s),
            load(gos_h, gos_v),
            load(gcnt_h, gcnt_s),
            load(params_h, par_v),
            load(est_h, est_v),
            load(mixed_h, mix_v),
        ]

    def multiply(h, turns):
        if turns[0] == 0:
            load_act[h].wait()
        left = cot_t[turns[0] * rows : (turns[-1] + 1) * rows, :]
        for first in range(0, tiles, 2):
            these = range(first, min(first + 2, tiles))
            right = act_v[h][:, pl.ds(first * LANES, len(these) * LANES)]
            grad = jnp.dot(left, right, preferred_element_type=jnp.float32) * scale
            if first == 0 and turns[0] == 0:
                load_mem[h][0].wait()
                if h == 0:
                    late.extend(later())
            for place, turn in enumerate(turns):
                base = pl.multiple_of(owner_at(turn) * own, 8)
                for j, c in enumerate(these):
                    view = pl.ds(base + c, rows, stride=tiles)
                    pend[h][view, :] = (
                        pend[h][view, :]
                        + grad[place * rows : (place + 1) * rows, j * LANES : (j + 1) * LANES]
                    )

    def gather(owner, h):
        blocks = pend[h].at[pl.ds(pl.multiple_of(owner * own, 8), own)]
        for k in range(cap):
            slots[h, owner, pl.ds(k, 1), :] = blocks[pl.ds(kept_s[owner, k], 1), :]

    sends = []
    for h in range(halves):
        sends.append([])
        for turns in parts:
            multiply(h, turns)
            if turns[0] == 0:
                load_mem[h][1].wait()
            if h == 0 and turns[0] == 0:
                load_kept_s.wait()
                enter()
            for turn in turns:
                owner = owner_at(turn)
                gather(owner, h)
                if turn < shards - 1:
                    copy = remote(
                        slots.at[h, owner], arrived.at[h, shard], send_sem.at[h, turn],
                        recv_sem.at[h, turn], (silo, owner),
                    )
                    copy.start()
                    sends[h].append(copy)
                else:
                    arrived[h, shard] = slots[h, shard]

    for copy in late:
        copy.wait()

    lane_cap = lax.broadcasted_iota(jnp.int32, (1, cap), 1)
    lane_gk = lax.broadcasted_iota(jnp.int32, (1, gk), 1)

    order = lax.broadcasted_iota(jnp.int32, (own, 1), 0)
    block_of = lax.rem(order, rows) * tiles + lax.div(order, rows)
    for pair in range(shards // 2):
        ids = []
        for source in (2 * pair, 2 * pair + 1):
            filled = lane_cap < kcnt_s[source, shard]
            ids.append(jnp.where(filled, kept_v[source, pl.ds(shard, 1), :], -1))
        ids = jnp.concatenate(ids, axis=1)
        onehot[:, pl.ds(pair * 2 * cap, 2 * cap)] = jnp.where(block_of == ids, 1.0, 0.0).astype(
            jnp.bfloat16
        )

    def gossip_hot(which):
        ids = jnp.where(lane_gk < gcnt_s[0, which], gos_v[which], -1)
        return jnp.where(block_of == ids, 1.0, 0.0)

    mine = gossip_hot(silo)
    ones = jnp.ones((gk, LANES), jnp.bfloat16)
    mask_own[...] = jnp.dot(mine.astype(jnp.bfloat16), ones, preferred_element_type=jnp.float32)
    gos_take[...] = mine.T.astype(jnp.bfloat16)
    gos_put[:, pl.ds(0, gk)] = gossip_hot(lower).astype(jnp.bfloat16)
    gos_put[:, pl.ds(gk, gk)] = gossip_hot(upper).astype(jnp.bfloat16)

    gos_mix[...] = jnp.dot(
        gos_take[...], onehot[...], preferred_element_type=jnp.float32
    ).astype(jnp.bfloat16)
    for h in range(halves):
        for c in range(tiles):
            part = pl.ds(c * rows, rows)
            high, low = split_pair(par_v[:, lanes_of(c, h)] - est_v[:, lanes_of(c, h)])
            drift_p[part, pl.ds(0, LANES)] = high
            drift_p[part, pl.ds(LANES, LANES)] = low
        taken = jnp.dot(gos_take[...], drift_p[...], preferred_element_type=jnp.float32)
        gos_base[h] = taken[:, :LANES] + taken[:, LANES:]

    goes = []

    def settle(h):
        for copy in sends[h]:
            copy.wait_recv()
        high, low = split_pair(arrived[h].reshape(shards * cap, LANES))
        pieces[h, :, pl.ds(0, LANES)] = high
        pieces[h, :, pl.ds(LANES, LANES)] = low
        taken = jnp.dot(gos_mix[...], pieces[h], preferred_element_type=jnp.float32)
        gos_send[h] = gos_base[h] - LEARN_RATE * (taken[:, :LANES] + taken[:, LANES:])
        for place, target in ((0, upper), (1, lower)):
            copy = remote(
                gos_send.at[h], gos_recv.at[h, place], gsend_sem.at[h, place],
                grecv_sem.at[h, place], (target, shard),
            )
            copy.start()
            goes.append(copy)

    def update(h):
        added = jnp.dot(onehot[...], pieces[h], preferred_element_type=jnp.float32)
        added = added[:, :LANES] + added[:, LANES:]
        for c in range(tiles):
            part = pl.ds(c * rows, rows)
            cols = lanes_of(c, h)
            half = par_v[:, cols] - LEARN_RATE * added[c * rows : (c + 1) * rows]
            delta = jnp.where(mask_own[part, :] > 0.0, half - est_v[:, cols], 0.0)
            estimate = est_v[:, cols] + delta
            est_o[:, cols] = estimate
            mix_v[:, cols] = mix_v[:, cols] + MIX_WEIGHT * delta
            par_v[:, cols] = half - CONSENSUS * estimate

    def close(h):
        for copy in goes[2 * h : 2 * h + 2]:
            copy.wait_recv()
        high, low = split_pair(gos_recv[h].reshape(2 * gk, LANES))
        gos_p[h, :, pl.ds(0, LANES)] = high
        gos_p[h, :, pl.ds(LANES, LANES)] = low
        near = jnp.dot(gos_put[...], gos_p[h], preferred_element_type=jnp.float32)
        near = near[:, :LANES] + near[:, LANES:]
        for c in range(tiles):
            cols = lanes_of(c, h)
            mixed = mix_v[:, cols] + MIX_WEIGHT * near[c * rows : (c + 1) * rows]
            mixed_o[:, cols] = mixed
            params_o[:, cols] = par_v[:, cols] + CONSENSUS * mixed

    ones_cap = jnp.ones((cap, LANES), jnp.bfloat16)
    place_of = lax.broadcasted_iota(jnp.int32, (own, 1), 0)

    def clear(owner, carry):
        ids = jnp.where(lane_cap < kcnt_s[shard, owner], kept_v[shard, pl.ds(owner, 1), :], -1)
        hit = jnp.where(place_of == ids, 1.0, 0.0).astype(jnp.bfloat16)
        kept = jnp.dot(hit, ones_cap, preferred_element_type=jnp.float32)
        base = pl.multiple_of(owner * own, 8)
        for h in range(halves):
            error_o[pl.ds(base, own), pl.ds(h * LANES, LANES)] = jnp.where(
                kept > 0.0, 0.0, pend[h][pl.ds(base, own), :]
            )
        return carry

    lax.fori_loop(0, shards, clear, 0)
    await_near()
    for h in range(halves):
        settle(h)
        update(h)
    for copy in [copy for group in sends for copy in group]:
        copy.wait_send()
    for h in range(halves):
        close(h)
    for copy in goes:
        copy.wait_send()


def finish(*refs):
    count = len(refs) // 2
    sems = refs[-1]
    copies = [
        pltpu.make_async_copy(refs[i], refs[count + i], sems.at[i]) for i in range(count)
    ]
    for copy in copies:
        copy.start()
    for copy in copies:
        copy.wait()


def body(
    activ, cotangent, error_memory, params, estimate, mixed,
    kept_blocks, kept_counts, gossip_blocks, gossip_counts,
):
    silos, shards = lax.axis_size("silo"), lax.axis_size("shard")
    tokens, width_in = activ.shape
    width_out = cotangent.shape[1]
    nblocks, block = error_memory.shape[2:]
    own = nblocks // shards
    cap, gk = kept_blocks.shape[3], gossip_blocks.shape[2]
    tiles = width_in // block
    halves = 2
    assert block == halves * LANES
    rows = own // tiles
    f32, bf16, i32 = jnp.float32, jnp.bfloat16, jnp.int32
    dims = (silos, shards, own, cap, gk, tiles, block)
    operands = (
        activ, cotangent, error_memory[0, 0], params[0], estimate[0], mixed[0],
        kept_blocks[0], kept_counts[0], gossip_blocks, gossip_counts.reshape(1, silos),
    )
    operands = tuple(pltpu.with_memory_space_constraint(x, pltpu.HBM) for x in operands)
    vmem = pltpu.VMEM
    outs = pl.pallas_call(
        functools.partial(kernel, dims),
        out_shape=(
            vmem((rows, width_in), f32),
            vmem((rows, width_in), f32),
            vmem((rows, width_in), f32),
            vmem((nblocks, block), f32),
        ),
        in_specs=[pl.BlockSpec(memory_space=pltpu.HBM)] * len(operands),
        out_specs=tuple([pl.BlockSpec(memory_space=pltpu.VMEM)] * 4),
        scratch_shapes=[
            vmem((tokens, tiles * LANES), bf16),
            vmem((tokens, tiles * LANES), bf16),
            vmem((tokens, width_out), bf16),
            vmem((width_out, tokens), bf16),
            vmem((nblocks, LANES), f32),
            vmem((nblocks, LANES), f32),
            vmem((halves, shards, cap, LANES), f32),
            vmem((halves, shards, cap, LANES), f32),
            vmem((halves, shards * cap, 2 * LANES), bf16),
            vmem((own, shards * cap), bf16),
            vmem((own, LANES), f32),
            vmem((gk, own), bf16),
            vmem((own, 2 * gk), bf16),
            vmem((gk, shards * cap), bf16),
            vmem((halves, gk, LANES), f32),
            vmem((own, 2 * LANES), bf16),
            vmem((halves, gk, LANES), f32),
            vmem((halves, 2, gk, LANES), f32),
            vmem((halves, 2 * gk, 2 * LANES), bf16),
            vmem((rows, width_in), f32),
            vmem((rows, width_in), f32),
            vmem((rows, width_in), f32),
            vmem((shards, shards, cap), i32),
            vmem((silos, 1, gk), i32),
            pltpu.SMEM((shards, cap), i32),
            pltpu.SMEM((shards, shards), i32),
            pltpu.SMEM((1, silos), i32),
            pltpu.SemaphoreType.DMA((2 + halves * 3 + 7,)),
            pltpu.SemaphoreType.DMA((halves, shards - 1)),
            pltpu.SemaphoreType.DMA((halves, shards - 1)),
            pltpu.SemaphoreType.DMA((halves, 2)),
            pltpu.SemaphoreType.DMA((halves, 2)),
            pltpu.SemaphoreType.REGULAR,
        ],
        compiler_params=pltpu.CompilerParams(
            collective_id=0, has_side_effects=True, vmem_limit_bytes=24 << 20
        ),
    )(*operands)
    outs = pl.pallas_call(
        finish,
        out_shape=tuple(jax.ShapeDtypeStruct(x.shape, x.dtype) for x in outs),
        in_specs=[pl.BlockSpec(memory_space=pltpu.VMEM)] * len(outs),
        out_specs=tuple([pl.BlockSpec(memory_space=pltpu.HBM)] * len(outs)),
        scratch_shapes=[pltpu.SemaphoreType.DMA((len(outs),))],
        compiler_params=pltpu.CompilerParams(vmem_limit_bytes=1 << 20),
    )(*outs)
    return (
        outs[0].reshape(params.shape),
        outs[1].reshape(estimate.shape),
        outs[2].reshape(mixed.shape),
        outs[3].reshape(error_memory.shape),
    )


def solution(mesh):
    in_specs = (
        P(("silo", "shard"), None),
        P(("silo", "shard"), None),
        P("silo", "shard", None, None),
        P("silo", "shard", None),
        P("silo", "shard", None),
        P("silo", "shard", None),
        P("silo", None, None, None),
        P("silo", None, None),
        P(None, "shard", None),
        P(None, "shard"),
    )
    out_specs = (
        P("silo", "shard", None),
        P("silo", "shard", None),
        P("silo", "shard", None),
        P("silo", "shard", None, None),
    )
    return jax.shard_map(body, mesh=mesh, in_specs=in_specs, out_specs=out_specs, check_vma=False)
```

```python
import functools

import jax
import jax.numpy as jnp
from jax import lax
from jax.experimental import pallas as pl
from jax.experimental.pallas import tpu as pltpu
from jax.sharding import PartitionSpec as P

LEARN_RATE = 0.25
CONSENSUS = 0.5
MIX_WEIGHT = 1.0 / 3.0
MESH = pl.DeviceIdType.MESH
LANES = 128


def split_pair(value):
    high = value.astype(jnp.bfloat16)
    low = (value - high.astype(jnp.float32)).astype(jnp.bfloat16)
    return high, low


def remote(src, dst, send, recv, target):
    return pltpu.make_async_remote_copy(
        src_ref=src, dst_ref=dst, send_sem=send, recv_sem=recv,
        device_id=target, device_id_type=MESH,
    )


def kernel(
    dims,
    activ_h, cot_h, mem_h, params_h, est_h, mixed_h, kept_h, kcnt_h, gos_h, gcnt_h,
    params_o, est_o, mixed_o, error_o,
    act_a, act_b, cot_v, cot_t, pend_a, pend_b, slots, arrived, pieces, onehot, mask_own, gos_take, gos_put, gos_mix, gos_base,
    drift_p, gos_send, gos_recv, gos_p, par_v, est_v, mix_v, kept_v, gos_v,
    kept_s, kcnt_s, gcnt_s,
    load_sem, send_sem, recv_sem, gsend_sem, grecv_sem, near_sem,
):
    silos, shards, own, cap, gk, tiles, block = dims
    rows = own // tiles
    act_v, pend = (act_a, act_b), (pend_a, pend_b)
    halves = len(pend)
    all_rows = rows * shards
    silo = lax.axis_index("silo")
    shard = lax.axis_index("shard")
    upper = lax.rem(silo + 1, silos)
    lower = lax.rem(silo + silos - 1, silos)
    scale = float(activ_h.shape[1]) ** -0.5
    pairs = shards // 2
    here, side = lax.div(shard, 2), lax.rem(shard, 2)

    def owner_at(turn):
        far = (turn + 1) % pairs
        return 2 * lax.rem(here + far, pairs) + (1 - side if turn < pairs else side)

    count = [0]

    def load(src, dst):
        copy = pltpu.make_async_copy(src, dst, load_sem.at[count[0]])
        count[0] += 1
        copy.start()
        return copy

    def lanes_of(c, h):
        return pl.ds(c * block + h * LANES, LANES)

    def load_all(copies, whole):
        sem = load_sem.at[count[0]]
        count[0] += 1
        for src, dst in copies:
            pltpu.make_async_copy(src, dst, sem).start()
        return pltpu.make_async_copy(whole[0], whole[1], sem)

    def load_half(h):
        return load_all(
            [
                (activ_h.at[:, lanes_of(c, h)], act_v[h].at[:, pl.ds(c * LANES, LANES)])
                for c in range(tiles)
            ],
            (activ_h.at[:, pl.ds(0, tiles * LANES)], act_v[h]),
        )

    def load_pend(h, turns):
        lanes = pl.ds(h * LANES, LANES)
        views = [pl.ds(pl.multiple_of(owner_at(turn) * own, 8), own) for turn in turns]
        whole = pl.ds(0, len(turns) * own)
        return load_all(
            [(mem_h.at[view, lanes], pend[h].at[view]) for view in views],
            (mem_h.at[whole, lanes], pend[h].at[whole]),
        )

    parts = (range(pairs), range(pairs, shards))
    load_cot = load(cot_h, cot_v)

    barrier = pltpu.get_barrier_semaphore()
    for turn in (1, 0, 2, 5, 3, 4, 6):
        pl.semaphore_signal(
            barrier, inc=1, device_id=(silo, owner_at(turn)), device_id_type=MESH
        )
    last = silos - 1

    @pl.when(silo != last)
    def _():
        pl.semaphore_signal(barrier, inc=1, device_id=(upper, shard), device_id_type=MESH)

    @pl.when(silo == 0)
    def _():
        pl.semaphore_signal(barrier, inc=1, device_id=(lower, shard), device_id_type=MESH)

    load_act = [load_half(0)]
    load_kept_s = load(kept_h.at[shard], kept_s)
    load_mem = [[load_pend(0, turns) for turns in parts]]

    def enter():
        greeted = jnp.where(silo == 0, 0, jnp.where(silo == last, 2, 1))
        pl.semaphore_wait(barrier, shards - 1 + greeted)

        @pl.when(silo != 0)
        def _():
            pl.semaphore_signal(near_sem, inc=1, device_id=(lower, shard), device_id_type=MESH)

        @pl.when(silo == last)
        def _():
            pl.semaphore_signal(near_sem, inc=1, device_id=(upper, shard), device_id_type=MESH)

    def await_near():
        @pl.when(silo != last)
        def _():
            pl.semaphore_wait(near_sem, jnp.where(silo == 0, 2, 1))

    load_cot.wait()
    turned = cot_v[...].T
    for owner in range(shards):
        turn = lax.rem(owner // 2 - here + 2 * pairs - 1, pairs) + jnp.where(
            side == owner % 2, pairs, 0
        )
        cot_t[pl.ds(pl.multiple_of(turn * rows, 16), rows), :] = turned[
            owner * rows : (owner + 1) * rows
        ]

    late = []

    def later():
        for h in range(1, halves):
            load_act.append(load_half(h))
            load_mem.append([load_pend(h, turns) for turns in parts])
        return [
            load(kept_h, kept_v),
            load(kcnt_h, kcnt_s),
            load(gos_h, gos_v),
            load(gcnt_h, gcnt_s),
            load(params_h, par_v),
            load(est_h, est_v),
            load(mixed_h, mix_v),
        ]

    def multiply(h, turns):
        if turns[0] == 0:
            load_act[h].wait()
        left = cot_t[turns[0] * rows : (turns[-1] + 1) * rows, :]
        for first in range(0, tiles, 2):
            these = range(first, min(first + 2, tiles))
            right = act_v[h][:, pl.ds(first * LANES, len(these) * LANES)]
            grad = jnp.dot(left, right, preferred_element_type=jnp.float32) * scale
            if first == 0 and turns[0] == 0:
                load_mem[h][0].wait()
                if h == 0:
                    late.extend(later())
            for place, turn in enumerate(turns):
                base = pl.multiple_of(owner_at(turn) * own, 8)
                for j, c in enumerate(these):
                    view = pl.ds(base + c, rows, stride=tiles)
                    pend[h][view, :] = (
                        pend[h][view, :]
                        + grad[place * rows : (place + 1) * rows, j * LANES : (j + 1) * LANES]
                    )

    def gather(owner, h):
        blocks = pend[h].at[pl.ds(pl.multiple_of(owner * own, 8), own)]
        for k in range(cap):
            slots[h, owner, pl.ds(k, 1), :] = blocks[pl.ds(kept_s[owner, k], 1), :]

    sends = []
    for h in range(halves):
        sends.append([])
        for turns in parts:
            multiply(h, turns)
            if turns[0] == 0:
                load_mem[h][1].wait()
            if h == 0 and turns[0] == 0:
                load_kept_s.wait()
                enter()
            for turn in turns:
                owner = owner_at(turn)
                gather(owner, h)
                if turn < shards - 1:
                    copy = remote(
                        slots.at[h, owner], arrived.at[h, shard], send_sem.at[h, turn],
                        recv_sem.at[h, turn], (silo, owner),
                    )
                    copy.start()
                    sends[h].append(copy)
                else:
                    arrived[h, shard] = slots[h, shard]

    for copy in late:
        copy.wait()

    lane_cap = lax.broadcasted_iota(jnp.int32, (1, cap), 1)
    lane_gk = lax.broadcasted_iota(jnp.int32, (1, gk), 1)

    order = lax.broadcasted_iota(jnp.int32, (own, 1), 0)
    block_of = lax.rem(order, rows) * tiles + lax.div(order, rows)
    for pair in range(shards // 2):
        ids = []
        for source in (2 * pair, 2 * pair + 1):
            filled = lane_cap < kcnt_s[source, shard]
            ids.append(jnp.where(filled, kept_v[source, pl.ds(shard, 1), :], -1))
        ids = jnp.concatenate(ids, axis=1)
        onehot[:, pl.ds(pair * 2 * cap, 2 * cap)] = jnp.where(block_of == ids, 1.0, 0.0).astype(
            jnp.bfloat16
        )

    def gossip_hot(which):
        ids = jnp.where(lane_gk < gcnt_s[0, which], gos_v[which], -1)
        return jnp.where(block_of == ids, 1.0, 0.0)

    mine = gossip_hot(silo)
    ones = jnp.ones((gk, LANES), jnp.bfloat16)
    mask_own[...] = jnp.dot(mine.astype(jnp.bfloat16), ones, preferred_element_type=jnp.float32)
    gos_take[...] = mine.T.astype(jnp.bfloat16)
    gos_put[:, pl.ds(0, gk)] = gossip_hot(lower).astype(jnp.bfloat16)
    gos_put[:, pl.ds(gk, gk)] = gossip_hot(upper).astype(jnp.bfloat16)

    gos_mix[...] = jnp.dot(
        gos_take[...], onehot[...], preferred_element_type=jnp.float32
    ).astype(jnp.bfloat16)
    for h in range(halves):
        for c in range(tiles):
            part = pl.ds(c * rows, rows)
            high, low = split_pair(par_v[:, lanes_of(c, h)] - est_v[:, lanes_of(c, h)])
            drift_p[part, pl.ds(0, LANES)] = high
            drift_p[part, pl.ds(LANES, LANES)] = low
        taken = jnp.dot(gos_take[...], drift_p[...], preferred_element_type=jnp.float32)
        gos_base[h] = taken[:, :LANES] + taken[:, LANES:]

    goes = []
    quarter = lax.rem(silo, 4)
    long_way = (quarter == 0) | (quarter == 3)

    def settle(h):
        for copy in sends[h]:
            copy.wait_recv()
        high, low = split_pair(arrived[h].reshape(shards * cap, LANES))
        pieces[h, :, pl.ds(0, LANES)] = high
        pieces[h, :, pl.ds(LANES, LANES)] = low
        taken = jnp.dot(gos_mix[...], pieces[h], preferred_element_type=jnp.float32)
        gos_send[h] = gos_base[h] - LEARN_RATE * (taken[:, :LANES] + taken[:, LANES:])
        odd = lax.rem(silo, 2)
        for place, target in (
            (1 - odd, jnp.where(odd == 1, upper, lower)),
            (odd, jnp.where(odd == 1, lower, upper)),
        ):
            goes.append(
                remote(
                    gos_send.at[h], gos_recv.at[h, place], gsend_sem.at[h, place],
                    grecv_sem.at[h, place], (target, shard),
                )
            )
        pl.when(long_way)(goes[2 * h].start)
        goes[2 * h + 1].start()

    def update(h):
        added = jnp.dot(onehot[...], pieces[h], preferred_element_type=jnp.float32)
        added = added[:, :LANES] + added[:, LANES:]
        for c in range(tiles):
            part = pl.ds(c * rows, rows)
            cols = lanes_of(c, h)
            half = par_v[:, cols] - LEARN_RATE * added[c * rows : (c + 1) * rows]
            delta = jnp.where(mask_own[part, :] > 0.0, half - est_v[:, cols], 0.0)
            estimate = est_v[:, cols] + delta
            est_o[:, cols] = estimate
            mix_v[:, cols] = mix_v[:, cols] + MIX_WEIGHT * delta
            par_v[:, cols] = half - CONSENSUS * estimate

    def close(h):
        for copy in goes[2 * h : 2 * h + 2]:
            copy.wait_recv()
        high, low = split_pair(gos_recv[h].reshape(2 * gk, LANES))
        gos_p[h, :, pl.ds(0, LANES)] = high
        gos_p[h, :, pl.ds(LANES, LANES)] = low
        near = jnp.dot(gos_put[...], gos_p[h], preferred_element_type=jnp.float32)
        near = near[:, :LANES] + near[:, LANES:]
        for c in range(tiles):
            cols = lanes_of(c, h)
            mixed = mix_v[:, cols] + MIX_WEIGHT * near[c * rows : (c + 1) * rows]
            mixed_o[:, cols] = mixed
            params_o[:, cols] = par_v[:, cols] + CONSENSUS * mixed

    ones_cap = jnp.ones((cap, LANES), jnp.bfloat16)
    place_of = lax.broadcasted_iota(jnp.int32, (own, 1), 0)

    def clear(owner, carry):
        ids = jnp.where(lane_cap < kcnt_s[shard, owner], kept_v[shard, pl.ds(owner, 1), :], -1)
        hit = jnp.where(place_of == ids, 1.0, 0.0).astype(jnp.bfloat16)
        kept = jnp.dot(hit, ones_cap, preferred_element_type=jnp.float32)
        base = pl.multiple_of(owner * own, 8)
        for h in range(halves):
            error_o[pl.ds(base, own), pl.ds(h * LANES, LANES)] = jnp.where(
                kept > 0.0, 0.0, pend[h][pl.ds(base, own), :]
            )
        return carry

    lax.fori_loop(0, shards, clear, 0)
    await_near()
    for h in range(halves):
        settle(h)
        update(h)
        pl.when(jnp.logical_not(long_way))(goes[2 * h].start)
    for copy in [copy for group in sends for copy in group]:
        copy.wait_send()
    for h in range(halves):
        close(h)
    for copy in goes:
        copy.wait_send()


def finish(*refs):
    count = len(refs) // 2
    sems = refs[-1]
    copies = [
        pltpu.make_async_copy(refs[i], refs[count + i], sems.at[i]) for i in range(count)
    ]
    for copy in copies:
        copy.start()
    for copy in copies:
        copy.wait()


def body(
    activ, cotangent, error_memory, params, estimate, mixed,
    kept_blocks, kept_counts, gossip_blocks, gossip_counts,
):
    silos, shards = lax.axis_size("silo"), lax.axis_size("shard")
    tokens, width_in = activ.shape
    width_out = cotangent.shape[1]
    nblocks, block = error_memory.shape[2:]
    own = nblocks // shards
    cap, gk = kept_blocks.shape[3], gossip_blocks.shape[2]
    tiles = width_in // block
    halves = 2
    assert block == halves * LANES
    rows = own // tiles
    f32, bf16, i32 = jnp.float32, jnp.bfloat16, jnp.int32
    dims = (silos, shards, own, cap, gk, tiles, block)
    operands = (
        activ, cotangent, error_memory[0, 0], params[0], estimate[0], mixed[0],
        kept_blocks[0], kept_counts[0], gossip_blocks, gossip_counts.reshape(1, silos),
    )
    operands = tuple(pltpu.with_memory_space_constraint(x, pltpu.HBM) for x in operands)
    vmem = pltpu.VMEM
    outs = pl.pallas_call(
        functools.partial(kernel, dims),
        out_shape=(
            vmem((rows, width_in), f32),
            vmem((rows, width_in), f32),
            vmem((rows, width_in), f32),
            vmem((nblocks, block), f32),
        ),
        in_specs=[pl.BlockSpec(memory_space=pltpu.HBM)] * len(operands),
        out_specs=tuple([pl.BlockSpec(memory_space=pltpu.VMEM)] * 4),
        scratch_shapes=[
            vmem((tokens, tiles * LANES), bf16),
            vmem((tokens, tiles * LANES), bf16),
            vmem((tokens, width_out), bf16),
            vmem((width_out, tokens), bf16),
            vmem((nblocks, LANES), f32),
            vmem((nblocks, LANES), f32),
            vmem((halves, shards, cap, LANES), f32),
            vmem((halves, shards, cap, LANES), f32),
            vmem((halves, shards * cap, 2 * LANES), bf16),
            vmem((own, shards * cap), bf16),
            vmem((own, LANES), f32),
            vmem((gk, own), bf16),
            vmem((own, 2 * gk), bf16),
            vmem((gk, shards * cap), bf16),
            vmem((halves, gk, LANES), f32),
            vmem((own, 2 * LANES), bf16),
            vmem((halves, gk, LANES), f32),
            vmem((halves, 2, gk, LANES), f32),
            vmem((halves, 2 * gk, 2 * LANES), bf16),
            vmem((rows, width_in), f32),
            vmem((rows, width_in), f32),
            vmem((rows, width_in), f32),
            vmem((shards, shards, cap), i32),
            vmem((silos, 1, gk), i32),
            pltpu.SMEM((shards, cap), i32),
            pltpu.SMEM((shards, shards), i32),
            pltpu.SMEM((1, silos), i32),
            pltpu.SemaphoreType.DMA((2 + halves * 3 + 7,)),
            pltpu.SemaphoreType.DMA((halves, shards - 1)),
            pltpu.SemaphoreType.DMA((halves, shards - 1)),
            pltpu.SemaphoreType.DMA((halves, 2)),
            pltpu.SemaphoreType.DMA((halves, 2)),
            pltpu.SemaphoreType.REGULAR,
        ],
        compiler_params=pltpu.CompilerParams(
            collective_id=0, has_side_effects=True, vmem_limit_bytes=24 << 20
        ),
    )(*operands)
    outs = pl.pallas_call(
        finish,
        out_shape=tuple(jax.ShapeDtypeStruct(x.shape, x.dtype) for x in outs),
        in_specs=[pl.BlockSpec(memory_space=pltpu.VMEM)] * len(outs),
        out_specs=tuple([pl.BlockSpec(memory_space=pltpu.HBM)] * len(outs)),
        scratch_shapes=[pltpu.SemaphoreType.DMA((len(outs),))],
        compiler_params=pltpu.CompilerParams(vmem_limit_bytes=1 << 20),
    )(*outs)
    return (
        outs[0].reshape(params.shape),
        outs[1].reshape(estimate.shape),
        outs[2].reshape(mixed.shape),
        outs[3].reshape(error_memory.shape),
    )


def solution(mesh):
    in_specs = (
        P(("silo", "shard"), None),
        P(("silo", "shard"), None),
        P("silo", "shard", None, None),
        P("silo", "shard", None),
        P("silo", "shard", None),
        P("silo", "shard", None),
        P("silo", None, None, None),
        P("silo", None, None),
        P(None, "shard", None),
        P(None, "shard"),
    )
    out_specs = (
        P("silo", "shard", None),
        P("silo", "shard", None),
        P("silo", "shard", None),
        P("silo", "shard", None, None),
    )
    return jax.shard_map(body, mesh=mesh, in_specs=in_specs, out_specs=out_specs, check_vma=False)
```
